32 devices in a mesh: row: 2 (over x), col: 16 (over z, y, core).
Axes of the slice: x: 2, y: 2, z: 4, core: 2. Of those that a mesh axis runs over, the one named last changes fastest.
Arguments:
- features: bfloat16 [64, 768, 256], P('row', 'col'), may hold values from -6 to 6
- conv_one: bfloat16 [3, 3, 256, 256], replicated, may hold values from -0.125 to 0.125
- bias_one: float32 [256], replicated, may hold values from -3 to 3
- conv_two: bfloat16 [3, 3, 256, 512], replicated, may hold values from -0.125 to 0.125
- bias_two: float32 [512], replicated, may hold values from -3 to 3
- conv_three: bfloat16 [16, 3, 3, 32, 32], P('col'), may hold values from -0.375 to 0.375
- bias_three: float32 [512], P('col'), may hold values from -3 to 3
Outputs:
- encoded: bfloat16 [32, 512, 384], P('row', 'col')
The draws below stay inside these ranges and needn't reach their ends.
All inputs are finite; a program needn't handle non-finite values.
Results may differ from the reference program's by a relative error of at most 0.0051.
Values may be sent and summed in bfloat16 or wider, within the bound.
A program may use at most 64 MiB of HBM per device.

```python
import jax
import jax.numpy as jnp
from jax import lax

C1 = 256
C2 = 512
GROUPS = 16
GW = 32
H1 = 64
W1 = 768


def block_scale(own_key, dims, pieces, low, top_value):
    level, own = 1.0, jax.random.fold_in(own_key, 6)
    for dim, parts in pieces:
        steps = jnp.exp(jax.random.uniform(jax.random.fold_in(own, dim), (parts,), jnp.float32, low / len(pieces), top_value / len(pieces)))
        level = level * jnp.repeat(steps, dims[dim] // parts).reshape([-1 if axis == dim else 1 for axis in range(len(dims))])
    return level


def gaussian(rng, shape, scale, limit, shards=(), dtype=jnp.bfloat16):
    result = scale * jax.random.normal(rng, shape, jnp.float32)
    if shards:
        result = result * block_scale(rng, shape, shards, -0.22, 0.18)
    return jnp.clip(result, -limit, limit).astype(dtype)


def setup_inputs(seed: int = 0) -> dict:
    splits = jax.random.split(jax.random.key(seed), 8)
    features = gaussian(splits[0], (H1, W1, C1), 1.0, 6.0, ((0, 2), (1, 16)))
    conv_one = gaussian(splits[1], (3, 3, C1, C1), (9 * C1) ** -0.5, 0.125)
    bias_one = gaussian(splits[2], (C1,), 0.5, 3.0, (), jnp.float32)
    conv_two = gaussian(splits[3], (3, 3, C1, C2), (9 * C1) ** -0.5, 0.125)
    bias_two = gaussian(splits[4], (C2,), 0.5, 3.0, (), jnp.float32)
    conv_three = gaussian(splits[5], (GROUPS, 3, 3, GW, GW), (9 * GW) ** -0.5, 0.375, ((0, 16),))
    bias_three = gaussian(splits[6], (C2,), 0.5, 3.0, ((0, 16),), jnp.float32)
    return {"features": features, "conv_one": conv_one, "bias_one": bias_one, "conv_two": conv_two, "bias_two": bias_two, "conv_three": conv_three, "bias_three": bias_three}


def convolve(inputs, kernel, stride, groups):
    return lax.conv_general_dilated(inputs, kernel, (stride, stride), ((1, 1), (1, 1)), dimension_numbers=("NHWC", "HWIO", "NHWC"), feature_group_count=groups, precision=lax.Precision.HIGHEST)


def reference(features, conv_one, bias_one, conv_two, bias_two, conv_three, bias_three):
    inputs = features.astype(jnp.float32)[None]
    summed = convolve(inputs, conv_one.astype(jnp.float32), 1, 1)
    layer_one = jax.nn.relu(summed + bias_one.astype(jnp.float32)).astype(jnp.bfloat16)
    summed = convolve(layer_one.astype(jnp.float32), conv_two.astype(jnp.float32), 2, 1)
    layer_two = jax.nn.relu(summed + bias_two.astype(jnp.float32)).astype(jnp.bfloat16)
    kernel = jnp.transpose(conv_three.astype(jnp.float32), (1, 2, 3, 0, 4)).reshape(3, 3, GW, GROUPS * GW)
    summed = convolve(layer_two.astype(jnp.float32), kernel, 1, GROUPS)
    summed = summed[0] + bias_three.astype(jnp.float32)
    return jnp.transpose(summed, (0, 2, 1)).astype(jnp.bfloat16)
```

```python
import functools

import jax
import jax.numpy as jnp
from jax import lax
from jax.experimental import pallas as pl
from jax.experimental.pallas import tpu as pltpu
from jax.sharding import PartitionSpec as P

MESH = pl.DeviceIdType.MESH
F32 = jnp.float32
BF16 = jnp.bfloat16


def dot(a, b):
    return jnp.dot(a, b, preferred_element_type=F32)


def kernel(
    rows, cols,
    feat_hbm, w1_hbm, b1_hbm, w2_hbm, b2_hbm, w3_hbm, b3_hbm, out,
    feat, w1, b1, w2, b2, w3, b3, x32, st_l, st_r, rc_l, rc_r, rc_u, rc_d, taps, a2, l2, send, main,
    high, low, top, bot, l32, shifted, band,
    w_sem, h_send, h_recv, m_send, m_recv, r_send, r_recv,
):
    row = lax.axis_index("row")
    col = lax.axis_index("col")
    tr, tc, ch = feat.shape
    half = tc // 2
    has_up, has_down = row > 0, row < rows - 1
    has_left, has_right = col > 0, col < cols - 1

    load_feat, load_w3, load_b3, load_b1, load_one, load_b2, load_two = [
        pltpu.make_async_copy(src, dst, w_sem.at[index])
        for index, (src, dst) in enumerate(
            (
                (feat_hbm, feat), (w3_hbm, w3), (b3_hbm, b3), (b1_hbm, b1),
                (w1_hbm, w1), (b2_hbm, b2), (w2_hbm, w2),
            )
        )
    ]
    load_feat.start()

    barrier = pltpu.get_barrier_semaphore()

    def greet(device_row, device_col):
        pl.semaphore_signal(barrier, inc=1, device_id=(device_row, device_col), device_id_type=MESH)

    reach = cols - 1
    for there, dr in ((has_up, -1), (has_down, 1)):
        for beside, dc in ((True, 0), (has_left, -1), (has_right, 1)):
            pl.when(there & beside)(functools.partial(greet, row + dr, col + dc))
            reach = reach + (there & beside).astype(jnp.int32)
    for k in range(1, cols):
        greet(row, lax.rem(col + k, cols))
    for load in (load_w3, load_b3, load_b1, load_one, load_b2, load_two):
        load.start()
    load_feat.wait()

    lanes_of = [slice(128 * h, 128 * h + 128) for h in range(ch // 128)]
    for h, part in enumerate(lanes_of):
        x32[h, 2 : tr + 2, 8 : tc + 8, :] = feat[:, :, part].astype(F32)
        st_r[:, :, part] = x32[h, 2 : tr + 2, tc + 6 : tc + 8, :].astype(BF16)
        st_l[:, :, part] = x32[h, 2 : tr + 2, 8:10, :].astype(BF16)
    zero = lambda ref, lo, hi: ref.__setitem__(
        slice(lo, hi), jnp.zeros((hi - lo,) + ref.shape[1:], ref.dtype)
    )
    copies = []
    plan = (
        (feat.at[tr - 2 : tr], rc_u, 1, 0, has_down, has_up, (rc_u, 0, 2)),
        (feat.at[0:1], rc_d, -1, 0, has_up, has_down, (rc_d, 0, 1)),
        (st_r, rc_l.at[2 : tr + 2], 0, 1, has_right, has_left, (rc_l, 2, tr + 2)),
        (st_l, rc_r.at[2 : tr + 2], 0, -1, has_left, has_right, (rc_r, 2, tr + 2)),
        (st_r.at[tr - 2 : tr], rc_l.at[0:2], 1, 1, has_down & has_right, has_up & has_left, (rc_l, 0, 2)),
        (st_r.at[0:1], rc_l.at[tr + 2 : tr + 3], -1, 1, has_up & has_right, has_down & has_left, (rc_l, tr + 2, tr + 3)),
        (st_l.at[tr - 2 : tr], rc_r.at[0:2], 1, -1, has_down & has_left, has_up & has_right, (rc_r, 0, 2)),
        (st_l.at[0:1], rc_r.at[tr + 2 : tr + 3], -1, -1, has_up & has_left, has_down & has_right, (rc_r, tr + 2, tr + 3)),
    )
    for index, (src, dst, dr, dc, sends, gets, hole) in enumerate(plan):
        copy = pltpu.make_async_remote_copy(
            src_ref=src, dst_ref=dst, send_sem=h_send.at[index], recv_sem=h_recv.at[index],
            device_id=(row + dr, col + dc), device_id_type=MESH,
        )
        copies.append(copy)
        pl.when(jnp.logical_not(gets))(functools.partial(zero, *hole))

    pl.semaphore_wait(barrier, reach)
    for copy, item in zip(copies, plan):
        pl.when(item[4])(copy.start)

    load_w3.wait()
    load_b3.wait()
    width = w3.shape[3]
    quad = 4 * width
    full = cols * half
    quarter = full // 4
    band[...] = jnp.zeros_like(band)
    for b in range(3):
        for a in range(3):
            block = w3[0, a, b]
            for i in range(4):
                at = (i + 3 + a) * width
                band[b, at : at + width, i * width : (i + 1) * width] = block
    bias3 = jnp.concatenate([b3[...]] * 4, axis=1)
    chunks = main.shape[0]
    for q in range(chunks + 2):
        l32[q, 0:8] = jnp.zeros((8, quad), F32)
        l32[q, full + 8 : full + 16] = jnp.zeros((8, quad), F32)
    for q in (0, chunks + 1):
        l32[q, 8 : full + 8] = jnp.zeros((full, quad), F32)

    for copy, item in zip(copies, plan):
        pl.when(item[5])(copy.wait_recv)
    for h, part in enumerate(lanes_of):
        x32[h, 0:2, 8 : tc + 8, :] = rc_u[:, :, part].astype(F32)
        x32[h, tr + 2 : tr + 3, 8 : tc + 8, :] = rc_d[:, :, part].astype(F32)
        x32[h, 0 : tr + 3, 6:8, :] = rc_l[:, :, part].astype(F32)
        x32[h, 0 : tr + 3, tc + 8 : tc + 10, :] = rc_r[:, :, part].astype(F32)

    for j in range(4):
        for r in range(0, tr + 4, 12):
            for h in range(ch // 128):
                taps[r : r + 12, :, j * ch + 128 * h : j * ch + 128 * h + 128] = x32[
                    h, r : r + 12, pl.ds(j + 6, 32, stride=2), :
                ].astype(BF16)

    load_b1.wait()
    load_one.wait()
    bias1 = b1[...]
    left_edge = jnp.logical_not(has_left)
    out_ch = w2.shape[3]

    def first_layer(first, pairs):
        m = pairs * 64
        for parity in range(2):
            acc = None
            for a in range(3):
                lhs = taps[pl.ds(2 * first + a, 2 * pairs), :, parity * ch : (parity + 3) * ch]
                part = dot(lhs.reshape(m, 3 * ch), w1[a].reshape(3 * ch, ch))
                acc = part if acc is None else acc + part
            acc = jnp.maximum(acc + bias1, 0.0)
            if parity == 0:
                spot = lax.broadcasted_iota(jnp.int32, acc.shape, 0)
                acc = jnp.where((lax.rem(spot, 32) == 0) & left_edge, 0.0, acc)
                moved = pltpu.roll(acc, m - 1, 0)
                a2[pl.ds(first, pairs), :, :, 2 * ch : 3 * ch] = moved.astype(BF16).reshape(pairs, 2, 32, ch)
            a2[pl.ds(first, pairs), :, :, parity * ch : (parity + 1) * ch] = acc.astype(BF16).reshape(
                pairs, 2, 32, ch
            )

    def second_layer(first, count):
        acc = None
        for a in range(3):
            lhs = a2[pl.ds(first + a // 2, count), a % 2].reshape(count * 32, 3 * ch)
            part = dot(lhs, w2[a].reshape(3 * ch, out_ch))
            acc = part if acc is None else acc + part
        l2[pl.ds(first, count)] = jnp.maximum(acc + b2[...], 0.0).reshape(count, 32, out_ch)

    def pack(p):
        for g in range(cols):
            piece = jnp.concatenate(
                [l2[4 * p + r, 0:half, g * width : (g + 1) * width] for r in range(4)], axis=1
            )
            send[p, g] = piece.astype(BF16)

    def main_copy(p, d):
        return pltpu.make_async_remote_copy(
            src_ref=send.at[p, d], dst_ref=main.at[p, col], send_sem=m_send.at[p],
            recv_sem=m_recv.at[p], device_id=(row, d), device_id_type=MESH,
        )

    def main_all(p):
        others = pl.ds(0, cols - 1)
        return pltpu.make_async_remote_copy(
            src_ref=send.at[p, others], dst_ref=main.at[p, others], send_sem=m_send.at[p],
            recv_sem=m_recv.at[p], device_id=(row, lax.rem(col + 1, cols)), device_id_type=MESH,
        )

    part = cols // 2
    own = col // part
    step = part // 2

    def send_out(p):
        for g in range(2):
            for k in range(step):
                main_copy(p, (1 - own) * part + g * step + lax.rem(col + k, step)).start()
        for k in range(1, part):
            main_copy(p, own * part + lax.rem(col + k, part)).start()
        main[p, col] = send[p, col]

    flip = has_down & jnp.logical_not(has_up)
    early = jnp.where(flip, chunks - 1, 0)
    late = chunks - 1 - early

    def clear_top():
        a2[0, 0] = jnp.zeros(a2.shape[2:], BF16)

    def emit(p):
        second_layer(4 * p, 4)
        pack(p)
        send_out(p)

    for p in range(1, chunks - 1):
        first_layer(4 * p + (p > 1), 4 + (p == 1))
        if p == 1:
            load_b2.wait()
            load_two.wait()
        emit(p)
    for p in (early, late):
        first_layer(4 * p + (p > 0), 4)
        pl.when(jnp.logical_not(has_up))(clear_top)
        emit(p)

    def relay_copy(dr):
        src, there, index = (high, top, 0) if dr > 0 else (low, bot, 1)
        return pltpu.make_async_remote_copy(
            src_ref=src, dst_ref=there, send_sem=r_send.at[index], recv_sem=r_recv.at[index],
            device_id=(row + dr, col), device_id_type=MESH,
        )

    def relay(dr):
        there, q, r = (high, chunks, 3) if dr > 0 else (low, 1, 0)
        pieces = [l32[q, 8 + quarter * t : 8 + quarter * (t + 1), r * width : (r + 1) * width] for t in range(4)]
        there[...] = jnp.concatenate(pieces, axis=1).astype(BF16)
        relay_copy(dr).start()

    def shift(q):
        for b in range(3):
            shifted[b, q] = l32[q, 7 + b : 7 + b + full].astype(BF16)

    def arrive(p):
        main_all(p).wait_recv()
        for s in range(cols):
            at = 8 + half * s
            l32[p + 1, at : at + half] = main[p, s].astype(F32)

    def edge_arrive(dr):
        relay_copy(dr).wait_recv()
        there, q, r = (top, 0, 3) if dr > 0 else (bot, chunks + 1, 0)
        for t in range(4):
            at = 8 + quarter * t
            l32[q, at : at + quarter, r * width : (r + 1) * width] = there[:, t * width : (t + 1) * width].astype(F32)

    def third_layer(q):
        acc = None
        for b in range(3):
            lhs = jnp.concatenate([shifted[b, q + t] for t in range(3)], axis=1)
            part = dot(lhs, band[b])
            acc = part if acc is None else acc + part
        out[pl.ds(4 * q, 4)] = (acc + bias3).T.reshape(4, width, full).astype(BF16)

    between = has_up & has_down
    for p in range(1, chunks - 1):
        arrive(p)
        shift(p + 1)
    arrive(early)
    pl.when(flip)(lambda: relay(1))
    pl.when(jnp.logical_not(flip) & has_up)(lambda: relay(-1))
    shift(early + 1)
    for q in range(2, chunks - 2):
        third_layer(q)
    third_layer(jnp.where(flip, chunks - 2, 1))

    @pl.when(between)
    def _():
        arrive(late)
        relay(1)

    pl.when(has_up)(lambda: edge_arrive(1))
    pl.when(has_down & jnp.logical_not(between))(lambda: edge_arrive(-1))
    shift(jnp.where(flip, chunks + 1, 0))
    third_layer(early)

    @pl.when(jnp.logical_not(between))
    def _():
        arrive(late)

    pl.when(between)(lambda: edge_arrive(-1))
    shift(late + 1)
    shift(jnp.where(flip, 0, chunks + 1))
    third_layer(jnp.where(flip, 1, chunks - 2))
    third_layer(late)

    for copy, item in zip(copies, plan):
        pl.when(item[4])(copy.wait_send)
    for p in range(chunks):
        main_all(p).wait_send()
    pl.when(has_down)(lambda: relay_copy(1).wait_send())
    pl.when(has_up)(lambda: relay_copy(-1).wait_send())


def on_device(rows, cols, features, conv_one, bias_one, conv_two, bias_two, conv_three, bias_three):
    tr, tc, ch = features.shape
    c2 = conv_two.shape[3]
    width = conv_three.shape[3]
    half, orow = tc // 2, tr // 2
    full, quad = cols * half, 4 * width
    vmem = pl.BlockSpec(memory_space=pltpu.VMEM)
    hbm = pl.BlockSpec(memory_space=pl.ANY)
    dma = pltpu.SemaphoreType.DMA
    return pl.pallas_call(
        functools.partial(kernel, rows, cols),
        out_shape=jax.ShapeDtypeStruct((orow, width, full), BF16),
        in_specs=[hbm] * 7,
        out_specs=vmem,
        scratch_shapes=[
            pltpu.VMEM(features.shape, BF16),
            pltpu.VMEM(conv_one.shape, BF16),
            pltpu.VMEM((1, ch), F32),
            pltpu.VMEM(conv_two.shape, BF16),
            pltpu.VMEM((1, c2), F32),
            pltpu.VMEM(conv_three.shape, BF16),
            pltpu.VMEM((1, width), F32),
            pltpu.VMEM((ch // 128, tr + 4, tc + 24, 128), F32),
            pltpu.VMEM((tr, 2, ch), BF16),
            pltpu.VMEM((tr, 2, ch), BF16),
            pltpu.VMEM((tr + 3, 2, ch), BF16),
            pltpu.VMEM((tr + 3, 2, ch), BF16),
            pltpu.VMEM((2, tc, ch), BF16),
            pltpu.VMEM((1, tc, ch), BF16),
            pltpu.VMEM((tr + 4, 32, 4 * ch), BF16),
            pltpu.VMEM((orow + 1, 2, 32, 3 * ch), BF16),
            pltpu.VMEM((orow, 32, c2), F32),
            pltpu.VMEM((orow // 4, cols, half, quad), BF16),
            pltpu.VMEM((orow // 4, cols, half, quad), BF16),
            pltpu.VMEM((full // 4, quad), BF16),
            pltpu.VMEM((full // 4, quad), BF16),
            pltpu.VMEM((full // 4, quad), BF16),
            pltpu.VMEM((full // 4, quad), BF16),
            pltpu.VMEM((orow // 4 + 2, full + 16, quad), F32),
            pltpu.VMEM((3, orow // 4 + 2, full, quad), BF16),
            pltpu.VMEM((3, 3 * quad, quad), BF16),
            dma((7,)), dma((8,)), dma((8,)), dma((orow // 4,)), dma((orow // 4,)), dma((2,)), dma((2,)),
        ],
        compiler_params=pltpu.CompilerParams(
            collective_id=0, has_side_effects=True, vmem_limit_bytes=60 * 1024 * 1024
        ),
    )(
        features, conv_one, bias_one.reshape(1, -1), conv_two, bias_two.reshape(1, -1),
        conv_three, bias_three.reshape(1, -1),
    )


def solution(mesh):
    in_specs = (
        P("row", "col", None),
        P(),
        P(),
        P(),
        P(),
        P("col", None, None, None, None),
        P("col"),
    )
    return jax.shard_map(
        functools.partial(on_device, mesh.shape["row"], mesh.shape["col"]),
        mesh=mesh, in_specs=in_specs, out_specs=P("row", "col", None), check_vma=False,
    )
```

```python
import functools

import jax
import jax.numpy as jnp
from jax import lax
from jax.experimental import pallas as pl
from jax.experimental.pallas import tpu as pltpu
from jax.sharding import PartitionSpec as P

MESH = pl.DeviceIdType.MESH
F32 = jnp.float32
BF16 = jnp.bfloat16


def dot(a, b):
    return jnp.dot(a, b, preferred_element_type=F32)


def kernel(
    rows, cols,
    feat_hbm, w1_hbm, b1_hbm, w2_hbm, b2_hbm, w3_hbm, shifted, band,
    feat, w1, b1, w2, b2, w3, x32, st_l, st_r, rc_l, rc_r, rc_u, rc_d, taps, a2, l2, send, main,
    high, low, top, bot, l32,
    w_sem, h_send, h_recv, m_send, m_recv, r_send, r_recv,
):
    row = lax.axis_index("row")
    col = lax.axis_index("col")
    tr, tc, ch = feat.shape
    half = tc // 2
    has_up, has_down = row > 0, row < rows - 1
    has_left, has_right = col > 0, col < cols - 1

    load_feat, load_w3, load_b1, load_one, load_b2, load_two = [
        pltpu.make_async_copy(src, dst, w_sem.at[index])
        for index, (src, dst) in enumerate(
            (
                (feat_hbm, feat), (w3_hbm, w3), (b1_hbm, b1),
                (w1_hbm, w1), (b2_hbm, b2), (w2_hbm, w2),
            )
        )
    ]
    load_feat.start()

    barrier = pltpu.get_barrier_semaphore()

    def greet(device_row, device_col):
        pl.semaphore_signal(barrier, inc=1, device_id=(device_row, device_col), device_id_type=MESH)

    reach = cols - 1
    for there, dr in ((has_up, -1), (has_down, 1)):
        for beside, dc in ((True, 0), (has_left, -1), (has_right, 1)):
            pl.when(there & beside)(functools.partial(greet, row + dr, col + dc))
            reach = reach + (there & beside).astype(jnp.int32)
    for k in range(1, cols):
        greet(row, lax.rem(col + k, cols))
    for load in (load_w3, load_b1, load_one, load_b2, load_two):
        load.start()
    load_feat.wait()

    lanes_of = [slice(128 * h, 128 * h + 128) for h in range(ch // 128)]
    for h, part in enumerate(lanes_of):
        x32[h, 2 : tr + 2, 8 : tc + 8, :] = feat[:, :, part].astype(F32)
        st_r[:, :, part] = x32[h, 2 : tr + 2, tc + 6 : tc + 8, :].astype(BF16)
        st_l[:, :, part] = x32[h, 2 : tr + 2, 8:10, :].astype(BF16)
    zero = lambda ref, lo, hi: ref.__setitem__(
        slice(lo, hi), jnp.zeros((hi - lo,) + ref.shape[1:], ref.dtype)
    )
    copies = []
    plan = (
        (feat.at[tr - 2 : tr], rc_u, 1, 0, has_down, has_up, (rc_u, 0, 2)),
        (feat.at[0:1], rc_d, -1, 0, has_up, has_down, (rc_d, 0, 1)),
        (st_r, rc_l.at[2 : tr + 2], 0, 1, has_right, has_left, (rc_l, 2, tr + 2)),
        (st_l, rc_r.at[2 : tr + 2], 0, -1, has_left, has_right, (rc_r, 2, tr + 2)),
        (st_r.at[tr - 2 : tr], rc_l.at[0:2], 1, 1, has_down & has_right, has_up & has_left, (rc_l, 0, 2)),
        (st_r.at[0:1], rc_l.at[tr + 2 : tr + 3], -1, 1, has_up & has_right, has_down & has_left, (rc_l, tr + 2, tr + 3)),
        (st_l.at[tr - 2 : tr], rc_r.at[0:2], 1, -1, has_down & has_left, has_up & has_right, (rc_r, 0, 2)),
        (st_l.at[0:1], rc_r.at[tr + 2 : tr + 3], -1, -1, has_up & has_left, has_down & has_right, (rc_r, tr + 2, tr + 3)),
    )
    for index, (src, dst, dr, dc, sends, gets, hole) in enumerate(plan):
        copy = pltpu.make_async_remote_copy(
            src_ref=src, dst_ref=dst, send_sem=h_send.at[index], recv_sem=h_recv.at[index],
            device_id=(row + dr, col + dc), device_id_type=MESH,
        )
        copies.append(copy)
        pl.when(jnp.logical_not(gets))(functools.partial(zero, *hole))

    pl.semaphore_wait(barrier, reach)
    for copy, item in zip(copies, plan):
        pl.when(item[4])(copy.start)

    load_w3.wait()
    width = w3.shape[3]
    quad = 4 * width
    full = cols * half
    quarter = full // 4
    band[...] = jnp.zeros_like(band)
    for b in range(3):
        for a in range(3):
            block = w3[0, a, b]
            for i in range(4):
                at = (i + 3 + a) * width
                band[b, at : at + width, i * width : (i + 1) * width] = block
    chunks = main.shape[0]
    for q in range(chunks + 2):
        l32[q, 0:8] = jnp.zeros((8, quad), F32)
        l32[q, full + 8 : full + 16] = jnp.zeros((8, quad), F32)
    for q in (0, chunks + 1):
        l32[q, 8 : full + 8] = jnp.zeros((full, quad), F32)

    for copy, item in zip(copies, plan):
        pl.when(item[5])(copy.wait_recv)
    for h, part in enumerate(lanes_of):
        x32[h, 0:2, 8 : tc + 8, :] = rc_u[:, :, part].astype(F32)
        x32[h, tr + 2 : tr + 3, 8 : tc + 8, :] = rc_d[:, :, part].astype(F32)
        x32[h, 0 : tr + 3, 6:8, :] = rc_l[:, :, part].astype(F32)
        x32[h, 0 : tr + 3, tc + 8 : tc + 10, :] = rc_r[:, :, part].astype(F32)

    for j in range(4):
        for r in range(0, tr + 4, 12):
            for h in range(ch // 128):
                taps[r : r + 12, :, j * ch + 128 * h : j * ch + 128 * h + 128] = x32[
                    h, r : r + 12, pl.ds(j + 6, 32, stride=2), :
                ].astype(BF16)

    load_b1.wait()
    load_one.wait()
    bias1 = b1[...]
    left_edge = jnp.logical_not(has_left)
    out_ch = w2.shape[3]

    def first_layer(first, pairs):
        m = pairs * 64
        for parity in range(2):
            acc = None
            for a in range(3):
                lhs = taps[pl.ds(2 * first + a, 2 * pairs), :, parity * ch : (parity + 3) * ch]
                part = dot(lhs.reshape(m, 3 * ch), w1[a].reshape(3 * ch, ch))
                acc = part if acc is None else acc + part
            acc = jnp.maximum(acc + bias1, 0.0)
            if parity == 0:
                spot = lax.broadcasted_iota(jnp.int32, acc.shape, 0)
                acc = jnp.where((lax.rem(spot, 32) == 0) & left_edge, 0.0, acc)
                moved = pltpu.roll(acc, m - 1, 0)
                a2[pl.ds(first, pairs), :, :, 2 * ch : 3 * ch] = moved.astype(BF16).reshape(pairs, 2, 32, ch)
            a2[pl.ds(first, pairs), :, :, parity * ch : (parity + 1) * ch] = acc.astype(BF16).reshape(
                pairs, 2, 32, ch
            )

    def second_layer(first, count):
        acc = None
        for a in range(3):
            lhs = a2[pl.ds(first + a // 2, count), a % 2].reshape(count * 32, 3 * ch)
            part = dot(lhs, w2[a].reshape(3 * ch, out_ch))
            acc = part if acc is None else acc + part
        l2[pl.ds(first, count)] = jnp.maximum(acc + b2[...], 0.0).reshape(count, 32, out_ch)

    def pack(p):
        for g in range(cols):
            piece = jnp.concatenate(
                [l2[4 * p + r, 0:half, g * width : (g + 1) * width] for r in range(4)], axis=1
            )
            send[p, g] = piece.astype(BF16)

    def main_copy(p, d):
        return pltpu.make_async_remote_copy(
            src_ref=send.at[p, d], dst_ref=main.at[p, col], send_sem=m_send.at[p],
            recv_sem=m_recv.at[p], device_id=(row, d), device_id_type=MESH,
        )

    def main_all(p):
        others = pl.ds(0, cols - 1)
        return pltpu.make_async_remote_copy(
            src_ref=send.at[p, others], dst_ref=main.at[p, others], send_sem=m_send.at[p],
            recv_sem=m_recv.at[p], device_id=(row, lax.rem(col + 1, cols)), device_id_type=MESH,
        )

    part = cols // 2
    own = col // part
    step = part // 2

    def send_out(p):
        for g in range(2):
            for k in range(step):
                main_copy(p, (1 - own) * part + g * step + lax.rem(col + k, step)).start()
        for k in range(1, part):
            main_copy(p, own * part + lax.rem(col + k, part)).start()
        main[p, col] = send[p, col]

    flip = has_down & jnp.logical_not(has_up)
    early = jnp.where(flip, chunks - 1, 0)
    late = chunks - 1 - early

    def clear_top():
        a2[0, 0] = jnp.zeros(a2.shape[2:], BF16)

    def emit(p):
        second_layer(4 * p, 4)
        pack(p)
        send_out(p)

    for p in range(1, chunks - 1):
        first_layer(4 * p + (p > 1), 4 + (p == 1))
        if p == 1:
            load_b2.wait()
            load_two.wait()
        emit(p)
    for p in (early, late):
        first_layer(4 * p + (p > 0), 4)
        pl.when(jnp.logical_not(has_up))(clear_top)
        emit(p)

    def relay_copy(dr):
        src, there, index = (high, top, 0) if dr > 0 else (low, bot, 1)
        return pltpu.make_async_remote_copy(
            src_ref=src, dst_ref=there, send_sem=r_send.at[index], recv_sem=r_recv.at[index],
            device_id=(row + dr, col), device_id_type=MESH,
        )

    def relay(dr):
        there, q, r = (high, chunks, 3) if dr > 0 else (low, 1, 0)
        pieces = [l32[q, 8 + quarter * t : 8 + quarter * (t + 1), r * width : (r + 1) * width] for t in range(4)]
        there[...] = jnp.concatenate(pieces, axis=1).astype(BF16)
        relay_copy(dr).start()

    def shift(q):
        for b in range(3):
            shifted[b, q] = l32[q, 7 + b : 7 + b + full].astype(BF16)

    def arrive(p):
        main_all(p).wait_recv()
        for s in range(cols):
            at = 8 + half * s
            l32[p + 1, at : at + half] = main[p, s].astype(F32)

    def edge_arrive(dr):
        relay_copy(dr).wait_recv()
        there, q, r = (top, 0, 3) if dr > 0 else (bot, chunks + 1, 0)
        for t in range(4):
            at = 8 + quarter * t
            l32[q, at : at + quarter, r * width : (r + 1) * width] = there[:, t * width : (t + 1) * width].astype(F32)

    between = has_up & has_down
    for p in range(1, chunks - 1):
        arrive(p)
        shift(p + 1)
    arrive(early)
    pl.when(flip)(lambda: relay(1))
    pl.when(jnp.logical_not(flip) & has_up)(lambda: relay(-1))
    shift(early + 1)
    shift(jnp.where(flip, 0, chunks + 1))
    pl.when(has_up & jnp.logical_not(between))(lambda: edge_arrive(1))
    pl.when(has_down & jnp.logical_not(between))(lambda: edge_arrive(-1))
    shift(jnp.where(flip, chunks + 1, 0))
    arrive(late)
    shift(late + 1)

    @pl.when(between)
    def _():
        relay(1)
        edge_arrive(1)
        edge_arrive(-1)
        shift(0)
        shift(chunks + 1)

    for copy, item in zip(copies, plan):
        pl.when(item[4])(copy.wait_send)
    for p in range(chunks):
        main_all(p).wait_send()
    pl.when(has_down)(lambda: relay_copy(1).wait_send())
    pl.when(has_up)(lambda: relay_copy(-1).wait_send())


def finish(shifted, band, b3, out):
    chunks, full, quad = shifted.shape[1] - 2, shifted.shape[2], shifted.shape[3]
    bias3 = jnp.concatenate([b3[...]] * 4, axis=1)
    for q in range(chunks):
        acc = None
        for b in range(3):
            lhs = jnp.concatenate([shifted[b, q + t] for t in range(3)], axis=1)
            part = dot(lhs, band[b])
            acc = part if acc is None else acc + part
        out[4 * q : 4 * q + 4] = (acc + bias3).T.reshape(4, quad // 4, full).astype(BF16)


def on_device(rows, cols, features, conv_one, bias_one, conv_two, bias_two, conv_three, bias_three):
    tr, tc, ch = features.shape
    c2 = conv_two.shape[3]
    width = conv_three.shape[3]
    half, orow = tc // 2, tr // 2
    full, quad = cols * half, 4 * width
    vmem = pl.BlockSpec(memory_space=pltpu.VMEM)
    hbm = pl.BlockSpec(memory_space=pltpu.HBM)
    dma = pltpu.SemaphoreType.DMA
    shifted, band = pl.pallas_call(
        functools.partial(kernel, rows, cols),
        out_shape=[
            pltpu.VMEM((3, orow // 4 + 2, full, quad), BF16),
            pltpu.VMEM((3, 3 * quad, quad), BF16),
        ],
        in_specs=[hbm] * 6,
        out_specs=[vmem, vmem],
        scratch_shapes=[
            pltpu.VMEM(features.shape, BF16),
            pltpu.VMEM(conv_one.shape, BF16),
            pltpu.VMEM((1, ch), F32),
            pltpu.VMEM(conv_two.shape, BF16),
            pltpu.VMEM((1, c2), F32),
            pltpu.VMEM(conv_three.shape, BF16),
            pltpu.VMEM((ch // 128, tr + 4, tc + 24, 128), F32),
            pltpu.VMEM((tr, 2, ch), BF16),
            pltpu.VMEM((tr, 2, ch), BF16),
            pltpu.VMEM((tr + 3, 2, ch), BF16),
            pltpu.VMEM((tr + 3, 2, ch), BF16),
            pltpu.VMEM((2, tc, ch), BF16),
            pltpu.VMEM((1, tc, ch), BF16),
            pltpu.VMEM((tr + 4, 32, 4 * ch), BF16),
            pltpu.VMEM((orow + 1, 2, 32, 3 * ch), BF16),
            pltpu.VMEM((orow, 32, c2), F32),
            pltpu.VMEM((orow // 4, cols, half, quad), BF16),
            pltpu.VMEM((orow // 4, cols, half, quad), BF16),
            pltpu.VMEM((full // 4, quad), BF16),
            pltpu.VMEM((full // 4, quad), BF16),
            pltpu.VMEM((full // 4, quad), BF16),
            pltpu.VMEM((full // 4, quad), BF16),
            pltpu.VMEM((orow // 4 + 2, full + 16, quad), F32),
            dma((6,)), dma((8,)), dma((8,)), dma((orow // 4,)), dma((orow // 4,)), dma((2,)), dma((2,)),
        ],
        compiler_params=pltpu.CompilerParams(
            collective_id=0, has_side_effects=True, vmem_limit_bytes=58 * 1024 * 1024
        ),
    )(
        features, conv_one, bias_one.reshape(1, -1), conv_two, bias_two.reshape(1, -1), conv_three,
    )
    return pl.pallas_call(
        finish,
        out_shape=jax.ShapeDtypeStruct((orow, width, full), BF16),
        in_specs=[vmem] * 3,
        out_specs=vmem,
        compiler_params=pltpu.CompilerParams(vmem_limit_bytes=24 * 1024 * 1024),
    )(shifted, band, bias_three.reshape(1, -1))


def solution(mesh):
    in_specs = (
        P("row", "col", None),
        P(),
        P(),
        P(),
        P(),
        P("col", None, None, None, None),
        P("col"),
    )
    return jax.shard_map(
        functools.partial(on_device, mesh.shape["row"], mesh.shape["col"]),
        mesh=mesh, in_specs=in_specs, out_specs=P("row", "col", None), check_vma=False,
    )
```

```python
import functools

import jax
import jax.numpy as jnp
from jax import lax
from jax.experimental import pallas as pl
from jax.experimental.pallas import tpu as pltpu
from jax.sharding import PartitionSpec as P

MESH = pl.DeviceIdType.MESH
F32 = jnp.float32
BF16 = jnp.bfloat16


def dot(a, b):
    return jnp.dot(a, b, preferred_element_type=F32)


def kernel(
    rows, cols,
    feat_hbm, w1_hbm, b1_hbm, w2_hbm, b2_hbm, w3_hbm, shifted, band,
    feat, w1, b1, w2, b2, w3, x32, st_l, st_r, rc_l, rc_r, rc_u, rc_d, taps, a2, l2, send, main,
    high, low, top, bot, l32,
    e32, a2e, l2e, send_e, main_e,
    w_sem, h_send, h_recv, m_send, m_recv, r_send, r_recv, e_send, e_recv,
):
    row = lax.axis_index("row")
    col = lax.axis_index("col")
    tr, tc, ch = feat.shape
    half = tc // 2
    has_up, has_down = row > 0, row < rows - 1
    has_left, has_right = col > 0, col < cols - 1

    load_feat, load_w3, load_b1, load_one, load_b2, load_two = [
        pltpu.make_async_copy(src, dst, w_sem.at[index])
        for index, (src, dst) in enumerate(
            (
                (feat_hbm, feat), (w3_hbm, w3), (b1_hbm, b1),
                (w1_hbm, w1), (b2_hbm, b2), (w2_hbm, w2),
            )
        )
    ]
    load_feat.start()

    barrier = pltpu.get_barrier_semaphore()

    def greet(device_row, device_col):
        pl.semaphore_signal(barrier, inc=1, device_id=(device_row, device_col), device_id_type=MESH)

    reach = cols - 1
    for there, dr in ((has_up, -1), (has_down, 1)):
        for beside, dc in ((True, 0), (has_left, -1), (has_right, 1)):
            pl.when(there & beside)(functools.partial(greet, row + dr, col + dc))
            reach = reach + (there & beside).astype(jnp.int32)
    for k in range(1, cols):
        greet(row, lax.rem(col + k, cols))
    for load in (load_b1, load_one, load_b2, load_two, load_w3):
        load.start()
    load_feat.wait()

    lanes_of = [slice(128 * h, 128 * h + 128) for h in range(ch // 128)]
    for h, part in enumerate(lanes_of):
        x32[h, 2 : tr + 2, 8 : tc + 8, :] = feat[:, :, part].astype(F32)
        st_r[:, :, part] = x32[h, 2 : tr + 2, tc + 6 : tc + 8, :].astype(BF16)
        st_l[:, :, part] = x32[h, 2 : tr + 2, 8:10, :].astype(BF16)
    zero = lambda ref, lo, hi: ref.__setitem__(
        slice(lo, hi), jnp.zeros((hi - lo,) + ref.shape[1:], ref.dtype)
    )
    copies = []
    plan = (
        (feat.at[tr - 2 : tr], rc_u, 1, 0, has_down, has_up, (rc_u, 0, 2)),
        (feat.at[0:1], rc_d, -1, 0, has_up, has_down, (rc_d, 0, 1)),
        (st_r, rc_l.at[2 : tr + 2], 0, 1, has_right, has_left, (rc_l, 2, tr + 2)),
        (st_l, rc_r.at[2 : tr + 2], 0, -1, has_left, has_right, (rc_r, 2, tr + 2)),
        (st_r.at[tr - 2 : tr], rc_l.at[0:2], 1, 1, has_down & has_right, has_up & has_left, (rc_l, 0, 2)),
        (st_r.at[0:1], rc_l.at[tr + 2 : tr + 3], -1, 1, has_up & has_right, has_down & has_left, (rc_l, tr + 2, tr + 3)),
        (st_l.at[tr - 2 : tr], rc_r.at[0:2], 1, -1, has_down & has_left, has_up & has_right, (rc_r, 0, 2)),
        (st_l.at[0:1], rc_r.at[tr + 2 : tr + 3], -1, -1, has_up & has_left, has_down & has_right, (rc_r, tr + 2, tr + 3)),
    )
    for index, (src, dst, dr, dc, sends, gets, hole) in enumerate(plan):
        copy = pltpu.make_async_remote_copy(
            src_ref=src, dst_ref=dst, send_sem=h_send.at[index], recv_sem=h_recv.at[index],
            device_id=(row + dr, col + dc), device_id_type=MESH,
        )
        copies.append(copy)
        pl.when(jnp.logical_not(gets))(functools.partial(zero, *hole))

    width = w3.shape[3]
    quad = 4 * width
    full = cols * half
    quarter = full // 4
    chunks = main.shape[0]

    def make_taps(first, count):
        for j in range(4):
            for h in range(ch // 128):
                taps[first : first + count, :, j * ch + 128 * h : j * ch + 128 * h + 128] = x32[
                    h, first : first + count, pl.ds(j + 6, 32, stride=2), :
                ].astype(BF16)

    inner = 8 * (chunks - 2)
    make_taps(8, inner + 4)

    load_b1.wait()
    load_one.wait()
    bias1 = b1[...]
    left_edge = jnp.logical_not(has_left)
    out_ch = w2.shape[3]

    def first_layer(first, pairs):
        m = pairs * 64
        for parity in range(2):
            acc = None
            for a in range(3):
                lhs = taps[pl.ds(2 * first + a, 2 * pairs), :, parity * ch : (parity + 3) * ch]
                part = dot(lhs.reshape(m, 3 * ch), w1[a].reshape(3 * ch, ch))
                acc = part if acc is None else acc + part
            acc = jnp.maximum(acc + bias1, 0.0)
            if parity == 0:
                spot = lax.broadcasted_iota(jnp.int32, acc.shape, 0)
                acc = jnp.where((lax.rem(spot, 32) == 0) & left_edge, 0.0, acc)
                moved = pltpu.roll(acc, m - 1, 0)
                a2[pl.ds(first, pairs), :, :, 2 * ch : 3 * ch] = moved.astype(BF16).reshape(pairs, 2, 32, ch)
            a2[pl.ds(first, pairs), :, :, parity * ch : (parity + 1) * ch] = acc.astype(BF16).reshape(
                pairs, 2, 32, ch
            )

    def second_layer(first, count):
        acc = None
        for a in range(3):
            lhs = a2[pl.ds(first + a // 2, count), a % 2].reshape(count * 32, 3 * ch)
            part = dot(lhs, w2[a].reshape(3 * ch, out_ch))
            acc = part if acc is None else acc + part
        l2[pl.ds(first, count)] = jnp.maximum(acc + b2[...], 0.0).reshape(count, 32, out_ch)

    def pack(p):
        for g in range(cols):
            piece = jnp.concatenate(
                [l2[4 * p + r, 0:half, g * width : (g + 1) * width] for r in range(4)], axis=1
            )
            send[p, g] = piece.astype(BF16)

    def main_copy(p, d):
        return pltpu.make_async_remote_copy(
            src_ref=send.at[p, d], dst_ref=main.at[p, col], send_sem=m_send.at[p],
            recv_sem=m_recv.at[p], device_id=(row, d), device_id_type=MESH,
        )

    def main_all(p):
        others = pl.ds(0, cols - 1)
        return pltpu.make_async_remote_copy(
            src_ref=send.at[p, others], dst_ref=main.at[p, others], send_sem=m_send.at[p],
            recv_sem=m_recv.at[p], device_id=(row, lax.rem(col + 1, cols)), device_id_type=MESH,
        )

    part = cols // 2
    own = col // part
    step = part // 2

    order = [(1 - own) * part + g * step + lax.rem(col + k, step) for g in range(2) for k in range(step)]
    order += [own * part + lax.rem(col + k, part) for k in range(1, part)]

    def send_out(p):
        for d in order:
            main_copy(p, d).start()
        main[p, col] = send[p, col]

    flip = has_down & jnp.logical_not(has_up)
    early = jnp.where(flip, chunks - 1, 0)
    late = chunks - 1 - early

    def clear_top():
        a2[0, 0] = jnp.zeros(a2.shape[2:], BF16)

    def emit(p):
        second_layer(4 * p, 4)
        pack(p)

    def edge_layers():
        base, picks = 8, 4
        far_j = 6 + 2 * (half + 1 - picks)
        for j in range(4):
            for h in range(ch // 128):
                lanes = slice(j * ch + 128 * h, j * ch + 128 * h + 128)
                for at, there in ((6, 0), (far_j, picks)):
                    e32[:, there : there + picks, lanes] = x32[
                        h, base : base + inner + 4, pl.ds(j + at, picks, stride=2), :
                    ]
        n = inner + 2
        m = n * 8
        for parity in range(2):
            acc = None
            for a in range(3):
                lhs = e32[a : a + n, :, parity * ch : (parity + 3) * ch].reshape(m, 3 * ch).astype(BF16)
                part = dot(lhs, w1[a].reshape(3 * ch, ch))
                acc = part if acc is None else acc + part
            acc = jnp.maximum(acc + bias1, 0.0)
            if parity == 0:
                spot = lax.broadcasted_iota(jnp.int32, acc.shape, 0)
                acc = jnp.where((lax.rem(spot, 8) == 0) & left_edge, 0.0, acc)
                a2e[:, :, :, 2 * ch : 3 * ch] = pltpu.roll(acc, m - 1, 0).reshape(n // 2, 2, 8, ch)
            a2e[:, :, :, parity * ch : (parity + 1) * ch] = acc.reshape(n // 2, 2, 8, ch)
        count = inner // 2
        acc = None
        for a in range(3):
            lhs = a2e[a // 2 : a // 2 + count, a % 2].reshape(count * 8, 3 * ch).astype(BF16)
            part = dot(lhs, w2[a].reshape(3 * ch, out_ch))
            acc = part if acc is None else acc + part
        l2e[...] = jnp.maximum(acc + b2[...], 0.0).reshape(count, 8, out_ch)
        for g in range(cols):
            lanes = slice(g * width, (g + 1) * width)
            lines = [
                jnp.concatenate([l2e[4 * p + r, j : j + 1, lanes] for r in range(4)], axis=1)
                for p in range(chunks - 2) for j in (0, 6)
            ]
            send_e[g] = jnp.concatenate(lines, axis=0).astype(BF16)

    def edge_copy(d):
        return pltpu.make_async_remote_copy(
            src_ref=send_e.at[d], dst_ref=main_e.at[col], send_sem=e_send, recv_sem=e_recv,
            device_id=(row, d), device_id_type=MESH,
        )

    def edge_all():
        others = pl.ds(0, cols - 1)
        return pltpu.make_async_remote_copy(
            src_ref=send_e.at[others], dst_ref=main_e.at[others], send_sem=e_send, recv_sem=e_recv,
            device_id=(row, lax.rem(col + 1, cols)), device_id_type=MESH,
        )

    def send_edges():
        for d in order:
            edge_copy(d).start()
        main_e[col] = send_e[col]

    for p in range(1, chunks - 1):
        first_layer(4 * p + (p > 1), 4 + (p == 1))
        if p == 1:
            pl.semaphore_wait(barrier, reach)
            for copy, item in zip(copies, plan):
                pl.when(item[4])(copy.start)
            load_b2.wait()
            load_two.wait()
        emit(p)
        send_out(p)

    load_w3.wait()
    band[...] = jnp.zeros_like(band)
    for b in range(3):
        for a in range(3):
            block = w3[0, a, b]
            for i in range(4):
                at = (i + 3 + a) * width
                band[b, at : at + width, i * width : (i + 1) * width] = block
    for q in range(chunks + 2):
        l32[q, 0:8] = jnp.zeros((8, quad), F32)
        l32[q, full + 8 : full + 16] = jnp.zeros((8, quad), F32)
    for q in (0, chunks + 1):
        l32[q, 8 : full + 8] = jnp.zeros((full, quad), F32)

    for copy, item in zip(copies, plan):
        pl.when(item[5])(copy.wait_recv)
    for h, part in enumerate(lanes_of):
        x32[h, 0:2, 8 : tc + 8, :] = rc_u[:, :, part].astype(F32)
        x32[h, tr + 2 : tr + 3, 8 : tc + 8, :] = rc_d[:, :, part].astype(F32)
        x32[h, 0 : tr + 3, 6:8, :] = rc_l[:, :, part].astype(F32)
        x32[h, 0 : tr + 3, tc + 8 : tc + 10, :] = rc_r[:, :, part].astype(F32)

    make_taps(0, 12)
    make_taps(inner + 8, 12)
    for p in (early, late):
        first_layer(4 * p, 5)
        pl.when(jnp.logical_not(has_up))(clear_top)
        emit(p)
        send_out(p)
        if p is early:
            edge_layers()
            send_edges()

    def relay_copy(dr):
        src, there, index = (high, top, 0) if dr > 0 else (low, bot, 1)
        return pltpu.make_async_remote_copy(
            src_ref=src, dst_ref=there, send_sem=r_send.at[index], recv_sem=r_recv.at[index],
            device_id=(row + dr, col), device_id_type=MESH,
        )

    def relay(dr):
        there, q, r = (high, chunks, 3) if dr > 0 else (low, 1, 0)
        pieces = [l32[q, 8 + quarter * t : 8 + quarter * (t + 1), r * width : (r + 1) * width] for t in range(4)]
        there[...] = jnp.concatenate(pieces, axis=1).astype(BF16)
        relay_copy(dr).start()

    def shift(q):
        for b in range(3):
            shifted[b, q] = l32[q, 7 + b : 7 + b + full].astype(BF16)

    def arrive(p):
        main_all(p).wait_recv()
        for s in range(cols):
            at = 8 + half * s
            l32[p + 1, at : at + half] = main[p, s].astype(F32)

    def edge_arrive(dr):
        relay_copy(dr).wait_recv()
        there, q, r = (top, 0, 3) if dr > 0 else (bot, chunks + 1, 0)
        for t in range(4):
            at = 8 + quarter * t
            l32[q, at : at + quarter, r * width : (r + 1) * width] = there[:, t * width : (t + 1) * width].astype(F32)

    between = has_up & has_down
    for p in range(1, chunks - 1):
        arrive(p)
    arrive(early)
    pl.when(flip)(lambda: relay(1))
    pl.when(jnp.logical_not(flip) & has_up)(lambda: relay(-1))
    shift(early + 1)
    shift(jnp.where(flip, 0, chunks + 1))
    edge_all().wait_recv()
    for s in range(cols):
        for p in range(1, chunks - 1):
            for k, j in enumerate((0, half - 1)):
                at = 8 + half * s + j
                l32[p + 1, at : at + 1] = main_e[s, 2 * (p - 1) + k : 2 * (p - 1) + k + 1].astype(F32)
    for p in range(1, chunks - 1):
        shift(p + 1)
    pl.when(has_up & jnp.logical_not(between))(lambda: edge_arrive(1))
    pl.when(has_down & jnp.logical_not(between))(lambda: edge_arrive(-1))
    shift(jnp.where(flip, chunks + 1, 0))
    arrive(late)
    shift(late + 1)

    @pl.when(between)
    def _():
        relay(1)
        edge_arrive(1)
        edge_arrive(-1)
        shift(0)
        shift(chunks + 1)

    for copy, item in zip(copies, plan):
        pl.when(item[4])(copy.wait_send)
    for p in range(chunks):
        main_all(p).wait_send()
    edge_all().wait_send()
    pl.when(has_down)(lambda: relay_copy(1).wait_send())
    pl.when(has_up)(lambda: relay_copy(-1).wait_send())


def finish(shifted, band, b3, out):
    chunks, full, quad = shifted.shape[1] - 2, shifted.shape[2], shifted.shape[3]
    bias3 = jnp.concatenate([b3[...]] * 4, axis=1)
    for q in range(chunks):
        acc = None
        for b in range(3):
            lhs = jnp.concatenate([shifted[b, q + t] for t in range(3)], axis=1)
            part = dot(lhs, band[b])
            acc = part if acc is None else acc + part
        out[4 * q : 4 * q + 4] = (acc + bias3).T.reshape(4, quad // 4, full).astype(BF16)


def on_device(rows, cols, features, conv_one, bias_one, conv_two, bias_two, conv_three, bias_three):
    tr, tc, ch = features.shape
    c2 = conv_two.shape[3]
    width = conv_three.shape[3]
    half, orow = tc // 2, tr // 2
    full, quad = cols * half, 4 * width
    vmem = pl.BlockSpec(memory_space=pltpu.VMEM)
    hbm = pl.BlockSpec(memory_space=pltpu.HBM)
    dma = pltpu.SemaphoreType.DMA
    shifted, band = pl.pallas_call(
        functools.partial(kernel, rows, cols),
        out_shape=[
            pltpu.VMEM((3, orow // 4 + 2, full, quad), BF16),
            pltpu.VMEM((3, 3 * quad, quad), BF16),
        ],
        in_specs=[hbm] * 6,
        out_specs=[vmem, vmem],
        scratch_shapes=[
            pltpu.VMEM(features.shape, BF16),
            pltpu.VMEM(conv_one.shape, BF16),
            pltpu.VMEM((1, ch), F32),
            pltpu.VMEM(conv_two.shape, BF16),
            pltpu.VMEM((1, c2), F32),
            pltpu.VMEM(conv_three.shape, BF16),
            pltpu.VMEM((ch // 128, tr + 4, tc + 24, 128), F32),
            pltpu.VMEM((tr, 2, ch), BF16),
            pltpu.VMEM((tr, 2, ch), BF16),
            pltpu.VMEM((tr + 3, 2, ch), BF16),
            pltpu.VMEM((tr + 3, 2, ch), BF16),
            pltpu.VMEM((2, tc, ch), BF16),
            pltpu.VMEM((1, tc, ch), BF16),
            pltpu.VMEM((tr + 4, 32, 4 * ch), BF16),
            pltpu.VMEM((orow + 1, 2, 32, 3 * ch), BF16),
            pltpu.VMEM((orow, 32, c2), F32),
            pltpu.VMEM((orow // 4, cols, half, quad), BF16),
            pltpu.VMEM((orow // 4, cols, half, quad), BF16),
            pltpu.VMEM((full // 4, quad), BF16),
            pltpu.VMEM((full // 4, quad), BF16),
            pltpu.VMEM((full // 4, quad), BF16),
            pltpu.VMEM((full // 4, quad), BF16),
            pltpu.VMEM((orow // 4 + 2, full + 16, quad), F32),
            pltpu.VMEM((tr - 12, 8, 4 * ch), F32),
            pltpu.VMEM((orow // 2 + 1, 2, 8, 3 * ch), F32),
            pltpu.VMEM((orow // 2, 8, c2), F32),
            pltpu.VMEM((cols, orow // 2 - 4, quad), BF16),
            pltpu.VMEM((cols, orow // 2 - 4, quad), BF16),
            dma((6,)), dma((8,)), dma((8,)), dma((orow // 4,)), dma((orow // 4,)), dma((2,)), dma((2,)), dma, dma,
        ],
        compiler_params=pltpu.CompilerParams(
            collective_id=0, has_side_effects=True, vmem_limit_bytes=58 * 1024 * 1024
        ),
    )(
        features, conv_one, bias_one.reshape(1, -1), conv_two, bias_two.reshape(1, -1), conv_three,
    )
    return pl.pallas_call(
        finish,
        out_shape=jax.ShapeDtypeStruct((orow, width, full), BF16),
        in_specs=[vmem] * 3,
        out_specs=vmem,
        compiler_params=pltpu.CompilerParams(vmem_limit_bytes=24 * 1024 * 1024),
    )(shifted, band, bias_three.reshape(1, -1))


def solution(mesh):
    in_specs = (
        P("row", "col", None),
        P(),
        P(),
        P(),
        P(),
        P("col", None, None, None, None),
        P("col"),
    )
    return jax.shard_map(
        functools.partial(on_device, mesh.shape["row"], mesh.shape["col"]),
        mesh=mesh, in_specs=in_specs, out_specs=P("row", "col", None), check_vma=False,
    )
```

```python
import functools

import jax
import jax.numpy as jnp
from jax import lax
from jax.experimental import pallas as pl
from jax.experimental.pallas import tpu as pltpu
from jax.sharding import PartitionSpec as P

MESH = pl.DeviceIdType.MESH
F32 = jnp.float32
BF16 = jnp.bfloat16


def dot(a, b):
    return jnp.dot(a, b, preferred_element_type=F32)


def kernel(
    rows, cols,
    feat_hbm, w1_hbm, b1_hbm, w2_hbm, b2_hbm, w3_hbm, shifted, band,
    feat, w1, b1, w2, b2, w3, x32, st_l, st_r, rc_l, rc_r, rc_u, rc_d, taps, a2, l2, send, main,
    high, low, top, bot, l32,
    e32, a2e, l2e, send_e, main_e,
    w_sem, h_send, h_recv, m_send, m_recv, r_send, r_recv, e_send, e_recv,
):
    row = lax.axis_index("row")
    col = lax.axis_index("col")
    tr, tc, ch = feat.shape
    half = tc // 2
    has_up, has_down = row > 0, row < rows - 1
    has_left, has_right = col > 0, col < cols - 1

    load_feat, load_w3, load_b1, load_one, load_b2, load_two = [
        pltpu.make_async_copy(src, dst, w_sem.at[index])
        for index, (src, dst) in enumerate(
            (
                (feat_hbm, feat), (w3_hbm, w3), (b1_hbm, b1),
                (w1_hbm, w1), (b2_hbm, b2), (w2_hbm, w2),
            )
        )
    ]
    load_feat.start()

    barrier = pltpu.get_barrier_semaphore()

    def greet(device_row, device_col):
        pl.semaphore_signal(barrier, inc=1, device_id=(device_row, device_col), device_id_type=MESH)

    reach = cols - 1
    for there, dr in ((has_up, -1), (has_down, 1)):
        for beside, dc in ((True, 0), (has_left, -1), (has_right, 1)):
            pl.when(there & beside)(functools.partial(greet, row + dr, col + dc))
            reach = reach + (there & beside).astype(jnp.int32)
    for k in range(1, cols):
        greet(row, lax.rem(col + k, cols))
    for load in (load_b1, load_one, load_b2, load_two, load_w3):
        load.start()
    load_feat.wait()

    lanes_of = [slice(128 * h, 128 * h + 128) for h in range(ch // 128)]
    for h, part in enumerate(lanes_of):
        x32[h, 2 : tr + 2, 8 : tc + 8, :] = feat[:, :, part].astype(F32)
        st_r[:, :, part] = x32[h, 2 : tr + 2, tc + 6 : tc + 8, :].astype(BF16)
        st_l[:, :, part] = x32[h, 2 : tr + 2, 8:10, :].astype(BF16)
    zero = lambda ref, lo, hi: ref.__setitem__(
        slice(lo, hi), jnp.zeros((hi - lo,) + ref.shape[1:], ref.dtype)
    )
    copies = []
    plan = (
        (feat.at[tr - 2 : tr], rc_u, 1, 0, has_down, has_up, (rc_u, 0, 2)),
        (feat.at[0:1], rc_d, -1, 0, has_up, has_down, (rc_d, 0, 1)),
        (st_r, rc_l.at[2 : tr + 2], 0, 1, has_right, has_left, (rc_l, 2, tr + 2)),
        (st_l, rc_r.at[2 : tr + 2], 0, -1, has_left, has_right, (rc_r, 2, tr + 2)),
        (st_r.at[tr - 2 : tr], rc_l.at[0:2], 1, 1, has_down & has_right, has_up & has_left, (rc_l, 0, 2)),
        (st_r.at[0:1], rc_l.at[tr + 2 : tr + 3], -1, 1, has_up & has_right, has_down & has_left, (rc_l, tr + 2, tr + 3)),
        (st_l.at[tr - 2 : tr], rc_r.at[0:2], 1, -1, has_down & has_left, has_up & has_right, (rc_r, 0, 2)),
        (st_l.at[0:1], rc_r.at[tr + 2 : tr + 3], -1, -1, has_up & has_left, has_down & has_right, (rc_r, tr + 2, tr + 3)),
    )
    for index, (src, dst, dr, dc, sends, gets, hole) in enumerate(plan):
        copy = pltpu.make_async_remote_copy(
            src_ref=src, dst_ref=dst, send_sem=h_send.at[index], recv_sem=h_recv.at[index],
            device_id=(row + dr, col + dc), device_id_type=MESH,
        )
        copies.append(copy)
        pl.when(jnp.logical_not(gets))(functools.partial(zero, *hole))

    width = w3.shape[3]
    quad = 4 * width
    full = cols * half
    quarter = full // 4
    chunks = main.shape[0]

    def make_taps(first, count):
        for j in range(4):
            for h in range(ch // 128):
                taps[first : first + count, :, j * ch + 128 * h : j * ch + 128 * h + 128] = x32[
                    h, first : first + count, pl.ds(j + 6, 32, stride=2), :
                ].astype(BF16)

    inner = 8 * (chunks - 2)
    make_taps(8, inner + 4)

    load_b1.wait()
    load_one.wait()
    bias1 = b1[...]
    left_edge = jnp.logical_not(has_left)
    out_ch = w2.shape[3]

    def first_layer(first, pairs):
        m = pairs * 64
        for parity in range(2):
            acc = None
            for a in range(3):
                lhs = taps[pl.ds(2 * first + a, 2 * pairs), :, parity * ch : (parity + 3) * ch]
                part = dot(lhs.reshape(m, 3 * ch), w1[a].reshape(3 * ch, ch))
                acc = part if acc is None else acc + part
            acc = jnp.maximum(acc + bias1, 0.0)
            if parity == 0:
                spot = lax.broadcasted_iota(jnp.int32, acc.shape, 0)
                acc = jnp.where((lax.rem(spot, 32) == 0) & left_edge, 0.0, acc)
                moved = pltpu.roll(acc, m - 1, 0)
                a2[pl.ds(first, pairs), :, :, 2 * ch : 3 * ch] = moved.astype(BF16).reshape(pairs, 2, 32, ch)
            a2[pl.ds(first, pairs), :, :, parity * ch : (parity + 1) * ch] = acc.astype(BF16).reshape(
                pairs, 2, 32, ch
            )

    def second_layer(first, count):
        acc = None
        for a in range(3):
            lhs = a2[pl.ds(first + a // 2, count), a % 2].reshape(count * 32, 3 * ch)
            part = dot(lhs, w2[a].reshape(3 * ch, out_ch))
            acc = part if acc is None else acc + part
        l2[pl.ds(first, count)] = jnp.maximum(acc + b2[...], 0.0).reshape(count, 32, out_ch)

    def pack(p):
        for g in range(cols):
            piece = jnp.concatenate(
                [l2[4 * p + r, 0:half, g * width : (g + 1) * width] for r in range(4)], axis=1
            )
            send[p, g] = piece.astype(BF16)

    def main_copy(p, d):
        return pltpu.make_async_remote_copy(
            src_ref=send.at[p, d], dst_ref=main.at[p, col], send_sem=m_send.at[p],
            recv_sem=m_recv.at[p], device_id=(row, d), device_id_type=MESH,
        )

    def main_all(p):
        others = pl.ds(0, cols - 1)
        return pltpu.make_async_remote_copy(
            src_ref=send.at[p, others], dst_ref=main.at[p, others], send_sem=m_send.at[p],
            recv_sem=m_recv.at[p], device_id=(row, lax.rem(col + 1, cols)), device_id_type=MESH,
        )

    part = cols // 2
    own = col // part

    zone = cols // 4
    mine = col // zone
    span = [[t * zone + lax.rem(col + k, 2) + 2 * (k // 2) for k in range(zone)] for t in (2 - 2 * own, 3 - 2 * own)]
    span.append([(2 * own + 1 - lax.rem(mine, 2)) * zone + lax.rem(col + k, 2) + 2 * (k // 2) for k in range(zone)])
    span.append([mine * zone + lax.rem(col + k, zone) for k in range(1, zone)])
    first_part, rest = span[0] + span[3], span[2] + span[1]

    def send_out(p, devices):
        for d in devices:
            main_copy(p, d).start()

    flip = has_down & jnp.logical_not(has_up)
    early = jnp.where(flip, chunks - 1, 0)
    late = chunks - 1 - early

    def clear_top():
        a2[0, 0] = jnp.zeros(a2.shape[2:], BF16)

    def emit(p):
        second_layer(4 * p, 4)
        pack(p)

    def edge_layers():
        base, picks = 8, 4
        far_j = 6 + 2 * (half + 1 - picks)
        for j in range(4):
            for h in range(ch // 128):
                lanes = slice(j * ch + 128 * h, j * ch + 128 * h + 128)
                for at, there in ((6, 0), (far_j, picks)):
                    e32[:, there : there + picks, lanes] = x32[
                        h, base : base + inner + 4, pl.ds(j + at, picks, stride=2), :
                    ]
        n = inner + 2
        m = n * 8
        for parity in range(2):
            acc = None
            for a in range(3):
                lhs = e32[a : a + n, :, parity * ch : (parity + 3) * ch].reshape(m, 3 * ch).astype(BF16)
                part = dot(lhs, w1[a].reshape(3 * ch, ch))
                acc = part if acc is None else acc + part
            acc = jnp.maximum(acc + bias1, 0.0)
            if parity == 0:
                spot = lax.broadcasted_iota(jnp.int32, acc.shape, 0)
                acc = jnp.where((lax.rem(spot, 8) == 0) & left_edge, 0.0, acc)
                a2e[:, :, :, 2 * ch : 3 * ch] = pltpu.roll(acc, m - 1, 0).reshape(n // 2, 2, 8, ch)
            a2e[:, :, :, parity * ch : (parity + 1) * ch] = acc.reshape(n // 2, 2, 8, ch)
        count = inner // 2
        acc = None
        for a in range(3):
            lhs = a2e[a // 2 : a // 2 + count, a % 2].reshape(count * 8, 3 * ch).astype(BF16)
            part = dot(lhs, w2[a].reshape(3 * ch, out_ch))
            acc = part if acc is None else acc + part
        l2e[...] = jnp.maximum(acc + b2[...], 0.0).reshape(count, 8, out_ch)
        for g in range(cols):
            lanes = slice(g * width, (g + 1) * width)
            lines = [
                jnp.concatenate([l2e[4 * p + r, j : j + 1, lanes] for r in range(4)], axis=1)
                for p in range(chunks - 2) for j in (0, 6)
            ]
            send_e[g] = jnp.concatenate(lines, axis=0).astype(BF16)

    def edge_copy(d):
        return pltpu.make_async_remote_copy(
            src_ref=send_e.at[d], dst_ref=main_e.at[col], send_sem=e_send, recv_sem=e_recv,
            device_id=(row, d), device_id_type=MESH,
        )

    def edge_all():
        others = pl.ds(0, cols - 1)
        return pltpu.make_async_remote_copy(
            src_ref=send_e.at[others], dst_ref=main_e.at[others], send_sem=e_send, recv_sem=e_recv,
            device_id=(row, lax.rem(col + 1, cols)), device_id_type=MESH,
        )

    def send_edges(devices):
        for d in devices:
            edge_copy(d).start()

    for p in range(1, chunks - 1):
        first_layer(4 * p + (p > 1), 4 + (p == 1))
        if p == 1:
            pl.semaphore_wait(barrier, reach)
            for copy, item in zip(copies, plan):
                pl.when(item[4])(copy.start)
            load_b2.wait()
            load_two.wait()
        emit(p)
        send_out(p, first_part + rest)
        main[p, col] = send[p, col]

    load_w3.wait()
    band[...] = jnp.zeros_like(band)
    for b in range(3):
        for a in range(3):
            block = w3[0, a, b]
            for i in range(8):
                at = (i + 3 + a) * width
                band[b, at : at + width, i * width : (i + 1) * width] = block
    for q in range(chunks + 2):
        l32[q, 0:8] = jnp.zeros((8, quad), F32)
        l32[q, full + 8 : full + 16] = jnp.zeros((8, quad), F32)
    for q in (0, chunks + 1):
        l32[q, 8 : full + 8] = jnp.zeros((full, quad), F32)

    for copy, item in zip(copies, plan):
        pl.when(item[5])(copy.wait_recv)
    for h, part in enumerate(lanes_of):
        x32[h, 0:2, 8 : tc + 8, :] = rc_u[:, :, part].astype(F32)
        x32[h, tr + 2 : tr + 3, 8 : tc + 8, :] = rc_d[:, :, part].astype(F32)
        x32[h, 0 : tr + 3, 6:8, :] = rc_l[:, :, part].astype(F32)
        x32[h, 0 : tr + 3, tc + 8 : tc + 10, :] = rc_r[:, :, part].astype(F32)

    make_taps(0, 12)
    make_taps(inner + 8, 12)
    for p in (early, late):
        first_layer(4 * p, 5)
        pl.when(jnp.logical_not(has_up))(clear_top)
        emit(p)
        send_out(p, first_part + rest)
        main[p, col] = send[p, col]
        if p is early:
            edge_layers()
            send_edges(first_part + rest)
            main_e[col] = send_e[col]

    def relay_copy(dr):
        src, there, index = (high, top, 0) if dr > 0 else (low, bot, 1)
        return pltpu.make_async_remote_copy(
            src_ref=src, dst_ref=there, send_sem=r_send.at[index], recv_sem=r_recv.at[index],
            device_id=(row + dr, col), device_id_type=MESH,
        )

    def relay(dr):
        there, q, r = (high, chunks, 3) if dr > 0 else (low, 1, 0)
        pieces = [l32[q, 8 + quarter * t : 8 + quarter * (t + 1), r * width : (r + 1) * width] for t in range(4)]
        there[...] = jnp.concatenate(pieces, axis=1).astype(BF16)
        relay_copy(dr).start()

    def shift(q):
        for b in range(3):
            shifted[b, q] = l32[q, 7 + b : 7 + b + full].astype(BF16)

    def arrive(p):
        main_all(p).wait_recv()
        for s in range(cols):
            at = 8 + half * s
            l32[p + 1, at : at + half] = main[p, s].astype(F32)

    def edge_arrive(dr):
        relay_copy(dr).wait_recv()
        there, q, r = (top, 0, 3) if dr > 0 else (bot, chunks + 1, 0)
        for t in range(4):
            at = 8 + quarter * t
            l32[q, at : at + quarter, r * width : (r + 1) * width] = there[:, t * width : (t + 1) * width].astype(F32)

    between = has_up & has_down
    arrive(1)
    arrive(early)
    pl.when(flip)(lambda: relay(1))
    pl.when(jnp.logical_not(flip) & has_up)(lambda: relay(-1))
    shift(early + 1)
    shift(jnp.where(flip, 0, chunks + 1))
    for p in range(2, chunks - 1):
        arrive(p)
    edge_all().wait_recv()
    for s in range(cols):
        for p in range(1, chunks - 1):
            for k, j in enumerate((0, half - 1)):
                at = 8 + half * s + j
                l32[p + 1, at : at + 1] = main_e[s, 2 * (p - 1) + k : 2 * (p - 1) + k + 1].astype(F32)
    for p in range(1, chunks - 1):
        shift(p + 1)
    pl.when(has_up & jnp.logical_not(between))(lambda: edge_arrive(1))
    pl.when(has_down & jnp.logical_not(between))(lambda: edge_arrive(-1))
    shift(jnp.where(flip, chunks + 1, 0))
    arrive(late)
    shift(late + 1)

    @pl.when(between)
    def _():
        relay(1)
        edge_arrive(1)
        edge_arrive(-1)
        shift(0)
        shift(chunks + 1)

    for copy, item in zip(copies, plan):
        pl.when(item[4])(copy.wait_send)
    for p in range(chunks):
        main_all(p).wait_send()
    edge_all().wait_send()
    pl.when(has_down)(lambda: relay_copy(1).wait_send())
    pl.when(has_up)(lambda: relay_copy(-1).wait_send())


def finish(shifted, band, b3, out):
    chunks, full, quad = shifted.shape[1] - 2, shifted.shape[2], shifted.shape[3]
    bias3 = jnp.concatenate([b3[...]] * 8, axis=1)
    for q in range(chunks // 2):
        acc = None
        for b in range(3):
            lhs = jnp.concatenate([shifted[b, 2 * q + t] for t in range(4)], axis=1)
            part = dot(lhs, band[b])
            acc = part if acc is None else acc + part
        out[8 * q : 8 * q + 8] = (acc + bias3).astype(BF16).T.reshape(8, quad // 4, full)


def on_device(rows, cols, features, conv_one, bias_one, conv_two, bias_two, conv_three, bias_three):
    tr, tc, ch = features.shape
    c2 = conv_two.shape[3]
    width = conv_three.shape[3]
    half, orow = tc // 2, tr // 2
    full, quad = cols * half, 4 * width
    vmem = pl.BlockSpec(memory_space=pltpu.VMEM)
    hbm = pl.BlockSpec(memory_space=pltpu.HBM)
    dma = pltpu.SemaphoreType.DMA
    shifted, band = pl.pallas_call(
        functools.partial(kernel, rows, cols),
        out_shape=[
            pltpu.VMEM((3, orow // 4 + 2, full, quad), BF16),
            pltpu.VMEM((3, 4 * quad, 2 * quad), BF16),
        ],
        in_specs=[hbm] * 6,
        out_specs=[vmem, vmem],
        scratch_shapes=[
            pltpu.VMEM(features.shape, BF16),
            pltpu.VMEM(conv_one.shape, BF16),
            pltpu.VMEM((1, ch), F32),
            pltpu.VMEM(conv_two.shape, BF16),
            pltpu.VMEM((1, c2), F32),
            pltpu.VMEM(conv_three.shape, BF16),
            pltpu.VMEM((ch // 128, tr + 4, tc + 24, 128), F32),
            pltpu.VMEM((tr, 2, ch), BF16),
            pltpu.VMEM((tr, 2, ch), BF16),
            pltpu.VMEM((tr + 3, 2, ch), BF16),
            pltpu.VMEM((tr + 3, 2, ch), BF16),
            pltpu.VMEM((2, tc, ch), BF16),
            pltpu.VMEM((1, tc, ch), BF16),
            pltpu.VMEM((tr + 4, 32, 4 * ch), BF16),
            pltpu.VMEM((orow + 1, 2, 32, 3 * ch), BF16),
            pltpu.VMEM((orow, 32, c2), F32),
            pltpu.VMEM((orow // 4, cols, half, quad), BF16),
            pltpu.VMEM((orow // 4, cols, half, quad), BF16),
            pltpu.VMEM((full // 4, quad), BF16),
            pltpu.VMEM((full // 4, quad), BF16),
            pltpu.VMEM((full // 4, quad), BF16),
            pltpu.VMEM((full // 4, quad), BF16),
            pltpu.VMEM((orow // 4 + 2, full + 16, quad), F32),
            pltpu.VMEM((tr - 12, 8, 4 * ch), F32),
            pltpu.VMEM((orow // 2 + 1, 2, 8, 3 * ch), F32),
            pltpu.VMEM((orow // 2, 8, c2), F32),
            pltpu.VMEM((cols, orow // 2 - 4, quad), BF16),
            pltpu.VMEM((cols, orow // 2 - 4, quad), BF16),
            dma((6,)), dma((8,)), dma((8,)), dma((orow // 4,)), dma((orow // 4,)), dma((2,)), dma((2,)), dma, dma,
        ],
        compiler_params=pltpu.CompilerParams(
            collective_id=0, has_side_effects=True, vmem_limit_bytes=58 * 1024 * 1024
        ),
    )(
        features, conv_one, bias_one.reshape(1, -1), conv_two, bias_two.reshape(1, -1), conv_three,
    )
    return pl.pallas_call(
        finish,
        out_shape=jax.ShapeDtypeStruct((orow, width, full), BF16),
        in_specs=[vmem] * 3,
        out_specs=vmem,
        compiler_params=pltpu.CompilerParams(vmem_limit_bytes=24 * 1024 * 1024),
    )(shifted, band, bias_three.reshape(1, -1))


def solution(mesh):
    in_specs = (
        P("row", "col", None),
        P(),
        P(),
        P(),
        P(),
        P("col", None, None, None, None),
        P("col"),
    )
    return jax.shard_map(
        functools.partial(on_device, mesh.shape["row"], mesh.shape["col"]),
        mesh=mesh, in_specs=in_specs, out_specs=P("row", "col", None), check_vma=False,
    )
```

```python
import functools

import jax
import jax.numpy as jnp
from jax import lax
from jax.experimental import pallas as pl
from jax.experimental.pallas import tpu as pltpu
from jax.sharding import PartitionSpec as P

MESH = pl.DeviceIdType.MESH
F32 = jnp.float32
BF16 = jnp.bfloat16


def dot(a, b):
    return jnp.dot(a, b, preferred_element_type=F32)


def kernel(
    rows, cols,
    feat_hbm, w1_hbm, b1_hbm, w2_hbm, b2_hbm, w3_hbm, shifted, band,
    feat, w1, b1, w2, b2, w3, x32, st_l, st_r, rc_l, rc_r, rc_u, rc_d, taps, a2, l2, send, main,
    high, low, top, bot, l32,
    e32, a2e, l2e, send_e, main_e,
    w_sem, h_send, h_recv, m_send, m_recv, r_send, r_recv, e_send, e_recv,
):
    row = lax.axis_index("row")
    col = lax.axis_index("col")
    tr, tc, ch = feat.shape
    half = tc // 2
    has_up, has_down = row > 0, row < rows - 1
    has_left, has_right = col > 0, col < cols - 1

    lo, hi = 6, 18
    load_mid, load_w3, load_b1, load_one, load_b2, load_two, load_low, load_high = [
        pltpu.make_async_copy(src, dst, w_sem.at[index])
        for index, (src, dst) in enumerate(
            (
                (feat_hbm.at[lo:hi], feat.at[lo:hi]), (w3_hbm, w3), (b1_hbm, b1),
                (w1_hbm, w1), (b2_hbm, b2), (w2_hbm, w2),
                (feat_hbm.at[0:lo], feat.at[0:lo]), (feat_hbm.at[hi:tr], feat.at[hi:tr]),
            )
        )
    ]
    load_mid.start()

    barrier = pltpu.get_barrier_semaphore()

    def greet(device_row, device_col):
        pl.semaphore_signal(barrier, inc=1, device_id=(device_row, device_col), device_id_type=MESH)

    reach = cols - 1
    for there, dr in ((has_up, -1), (has_down, 1)):
        for beside, dc in ((True, 0), (has_left, -1), (has_right, 1)):
            pl.when(there & beside)(functools.partial(greet, row + dr, col + dc))
            reach = reach + (there & beside).astype(jnp.int32)
    for k in range(1, cols):
        greet(row, lax.rem(col + k, cols))
    for load in (load_one, load_b1, load_low, load_high):
        load.start()
    lanes_of = [slice(128 * h, 128 * h + 128) for h in range(ch // 128)]

    def widen(first, last):
        for h, part in enumerate(lanes_of):
            x32[h, first + 2 : last + 2, 8 : tc + 8, :] = feat[first:last, :, part].astype(F32)

    def make_taps(first, count):
        for j in range(4):
            for h in range(ch // 128):
                taps[pl.ds(first, count), :, j * ch + 128 * h : j * ch + 128 * h + 128] = x32[
                    h, pl.ds(first, count), pl.ds(j + 6, 32, stride=2), :
                ].astype(BF16)

    load_mid.wait()
    for load in (load_b2, load_two, load_w3):
        load.start()
    widen(lo, hi)
    make_taps(lo + 2, hi - lo)

    zero = lambda ref, lo, hi: ref.__setitem__(
        slice(lo, hi), jnp.zeros((hi - lo,) + ref.shape[1:], ref.dtype)
    )
    copies = []
    plan = (
        (feat.at[tr - 2 : tr], rc_u, 1, 0, has_down, has_up, (rc_u, 0, 2)),
        (feat.at[0:1], rc_d, -1, 0, has_up, has_down, (rc_d, 0, 1)),
        (st_r, rc_l.at[2 : tr + 2], 0, 1, has_right, has_left, (rc_l, 2, tr + 2)),
        (st_l, rc_r.at[2 : tr + 2], 0, -1, has_left, has_right, (rc_r, 2, tr + 2)),
        (st_r.at[tr - 2 : tr], rc_l.at[0:2], 1, 1, has_down & has_right, has_up & has_left, (rc_l, 0, 2)),
        (st_r.at[0:1], rc_l.at[tr + 2 : tr + 3], -1, 1, has_up & has_right, has_down & has_left, (rc_l, tr + 2, tr + 3)),
        (st_l.at[tr - 2 : tr], rc_r.at[0:2], 1, -1, has_down & has_left, has_up & has_right, (rc_r, 0, 2)),
        (st_l.at[0:1], rc_r.at[tr + 2 : tr + 3], -1, -1, has_up & has_left, has_down & has_right, (rc_r, tr + 2, tr + 3)),
    )
    for index, (src, dst, dr, dc, sends, gets, hole) in enumerate(plan):
        copy = pltpu.make_async_remote_copy(
            src_ref=src, dst_ref=dst, send_sem=h_send.at[index], recv_sem=h_recv.at[index],
            device_id=(row + dr, col + dc), device_id_type=MESH,
        )
        copies.append(copy)
        pl.when(jnp.logical_not(gets))(functools.partial(zero, *hole))

    width = w3.shape[3]
    quad = 4 * width
    full = cols * half
    quarter = full // 4
    chunks = main.shape[0]

    inner = 8 * (chunks - 2)
    load_b1.wait()
    load_one.wait()
    bias1 = b1[...]
    left_edge = jnp.logical_not(has_left)
    out_ch = w2.shape[3]

    def first_layer(first, lines):
        m = lines * 32
        for parity in range(2):
            acc = None
            for a in range(3):
                lhs = taps[pl.ds(first + a, lines), :, parity * ch : (parity + 3) * ch]
                part = dot(lhs.reshape(m, 3 * ch), w1[a].reshape(3 * ch, ch))
                acc = part if acc is None else acc + part
            acc = jnp.maximum(acc + bias1, 0.0)
            if parity == 0:
                spot = lax.broadcasted_iota(jnp.int32, acc.shape, 0)
                acc = jnp.where((lax.rem(spot, 32) == 0) & left_edge, 0.0, acc)
                moved = pltpu.roll(acc, m - 1, 0)
                a2[pl.ds(first, lines), :, 2 * ch : 3 * ch] = moved.astype(BF16).reshape(lines, 32, ch)
            a2[pl.ds(first, lines), :, parity * ch : (parity + 1) * ch] = acc.astype(BF16).reshape(lines, 32, ch)

    def second_layer(first, count):
        acc = None
        for a in range(3):
            lhs = jnp.concatenate([a2[2 * (first + i) + a] for i in range(count)], axis=0)
            part = dot(lhs, w2[a].reshape(3 * ch, out_ch))
            acc = part if acc is None else acc + part
        l2[pl.ds(first, count)] = jnp.maximum(acc + b2[...], 0.0).reshape(count, 32, out_ch)

    def pack(p):
        for g in range(cols):
            piece = jnp.concatenate(
                [l2[4 * p + r, 0:half, g * width : (g + 1) * width] for r in range(4)], axis=1
            )
            send[p, g] = piece.astype(BF16)

    def main_copy(p, d):
        return pltpu.make_async_remote_copy(
            src_ref=send.at[p, d], dst_ref=main.at[p, col], send_sem=m_send.at[p],
            recv_sem=m_recv.at[p], device_id=(row, d), device_id_type=MESH,
        )

    def main_all(p):
        others = pl.ds(0, cols - 1)
        return pltpu.make_async_remote_copy(
            src_ref=send.at[p, others], dst_ref=main.at[p, others], send_sem=m_send.at[p],
            recv_sem=m_recv.at[p], device_id=(row, lax.rem(col + 1, cols)), device_id_type=MESH,
        )

    part = cols // 2
    own = col // part

    zone = cols // 4
    mine = col // zone
    span = [[t * zone + lax.rem(col + k, 2) + 2 * (k // 2) for k in range(zone)] for t in (2 - 2 * own, 3 - 2 * own)]
    span.append([(2 * own + 1 - lax.rem(mine, 2)) * zone + lax.rem(col + k, 2) + 2 * (k // 2) for k in range(zone)])
    span.append([mine * zone + lax.rem(col + k, zone) for k in range(1, zone)])
    first_part, rest = span[0] + span[3], span[2] + span[1]

    def send_out(p, devices):
        for d in devices:
            main_copy(p, d).start()

    flip = has_down & jnp.logical_not(has_up)
    early = jnp.where(flip, chunks - 1, 0)
    late = chunks - 1 - early

    def clear_top():
        a2[0] = jnp.zeros(a2.shape[1:], BF16)

    def emit(p):
        second_layer(4 * p, 4)
        pack(p)

    def edge_layers():
        base, picks = 8, 4
        far_j = 6 + 2 * (half + 1 - picks)
        for j in range(4):
            for h in range(ch // 128):
                lanes = slice(j * ch + 128 * h, j * ch + 128 * h + 128)
                for at, there in ((6, 0), (far_j, picks)):
                    e32[:, there : there + picks, lanes] = x32[
                        h, base : base + inner + 4, pl.ds(j + at, picks, stride=2), :
                    ]
        n = inner + 2
        m = n * 8
        for parity in range(2):
            acc = None
            for a in range(3):
                lhs = e32[a : a + n, :, parity * ch : (parity + 3) * ch].reshape(m, 3 * ch).astype(BF16)
                part = dot(lhs, w1[a].reshape(3 * ch, ch))
                acc = part if acc is None else acc + part
            acc = jnp.maximum(acc + bias1, 0.0)
            if parity == 0:
                spot = lax.broadcasted_iota(jnp.int32, acc.shape, 0)
                acc = jnp.where((lax.rem(spot, 8) == 0) & left_edge, 0.0, acc)
                a2e[:, :, :, 2 * ch : 3 * ch] = pltpu.roll(acc, m - 1, 0).reshape(n // 2, 2, 8, ch)
            a2e[:, :, :, parity * ch : (parity + 1) * ch] = acc.reshape(n // 2, 2, 8, ch)
        count = inner // 2
        acc = None
        for a in range(3):
            lhs = a2e[a // 2 : a // 2 + count, a % 2].reshape(count * 8, 3 * ch).astype(BF16)
            part = dot(lhs, w2[a].reshape(3 * ch, out_ch))
            acc = part if acc is None else acc + part
        l2e[...] = jnp.maximum(acc + b2[...], 0.0).reshape(count, 8, out_ch)
        for g in range(cols):
            lanes = slice(g * width, (g + 1) * width)
            lines = [
                jnp.concatenate([l2e[4 * p + r, j : j + 1, lanes] for r in range(4)], axis=1)
                for p in range(chunks - 2) for j in (0, 6)
            ]
            send_e[g] = jnp.concatenate(lines, axis=0).astype(BF16)

    def edge_copy(d):
        return pltpu.make_async_remote_copy(
            src_ref=send_e.at[d], dst_ref=main_e.at[col], send_sem=e_send, recv_sem=e_recv,
            device_id=(row, d), device_id_type=MESH,
        )

    def edge_all():
        others = pl.ds(0, cols - 1)
        return pltpu.make_async_remote_copy(
            src_ref=send_e.at[others], dst_ref=main_e.at[others], send_sem=e_send, recv_sem=e_recv,
            device_id=(row, lax.rem(col + 1, cols)), device_id_type=MESH,
        )

    def send_edges(devices):
        for d in devices:
            edge_copy(d).start()

    for p in range(1, chunks - 1):
        if p > 1:
            make_taps(hi + 2 + 8 * (p - 2), 8)
        first_layer(8 * p + (p > 1), 8 + (p == 1))
        if p == 1:
            load_low.wait()
            load_high.wait()
            widen(0, lo)
            widen(hi, tr)
            for h, part in enumerate(lanes_of):
                st_r[:, :, part] = x32[h, 2 : tr + 2, tc + 6 : tc + 8, :].astype(BF16)
                st_l[:, :, part] = x32[h, 2 : tr + 2, 8:10, :].astype(BF16)
            pl.semaphore_wait(barrier, reach)
            for copy, item in zip(copies, plan):
                pl.when(item[4])(copy.start)
            load_b2.wait()
            load_two.wait()
        emit(p)
        send_out(p, first_part + rest)
        main[p, col] = send[p, col]

    for copy, item in zip(copies, plan):
        pl.when(item[5])(copy.wait_recv)
    for h, part in enumerate(lanes_of):
        x32[h, 0:2, 8 : tc + 8, :] = rc_u[:, :, part].astype(F32)
        x32[h, tr + 2 : tr + 3, 8 : tc + 8, :] = rc_d[:, :, part].astype(F32)
        x32[h, 0 : tr + 3, 6:8, :] = rc_l[:, :, part].astype(F32)
        x32[h, 0 : tr + 3, tc + 8 : tc + 10, :] = rc_r[:, :, part].astype(F32)

    for p in (early, late):
        make_taps(8 * p, 12)
        first_layer(8 * p, 9)
        pl.when(jnp.logical_not(has_up))(clear_top)
        emit(p)
        send_out(p, first_part + rest)
        main[p, col] = send[p, col]
        if p is early:
            edge_layers()
            send_edges(first_part + rest)
            main_e[col] = send_e[col]

    load_w3.wait()
    band[...] = jnp.zeros_like(band)
    for b in range(3):
        for a in range(3):
            block = w3[0, a, b]
            for i in range(8):
                at = (i + 3 + a) * width
                band[b, at : at + width, i * width : (i + 1) * width] = block
    for q in range(chunks + 2):
        l32[q, 0:8] = jnp.zeros((8, quad), F32)
        l32[q, full + 8 : full + 16] = jnp.zeros((8, quad), F32)
    for q in (0, chunks + 1):
        l32[q, 8 : full + 8] = jnp.zeros((full, quad), F32)


    def relay_copy(dr):
        src, there, index = (high, top, 0) if dr > 0 else (low, bot, 1)
        return pltpu.make_async_remote_copy(
            src_ref=src, dst_ref=there, send_sem=r_send.at[index], recv_sem=r_recv.at[index],
            device_id=(row + dr, col), device_id_type=MESH,
        )

    def relay(dr):
        there, q, r = (high, chunks, 3) if dr > 0 else (low, 1, 0)
        pieces = [l32[q, 8 + quarter * t : 8 + quarter * (t + 1), r * width : (r + 1) * width] for t in range(4)]
        there[...] = jnp.concatenate(pieces, axis=1).astype(BF16)
        relay_copy(dr).start()

    def shift(q):
        for b in range(3):
            shifted[b, q] = l32[q, 7 + b : 7 + b + full].astype(BF16)

    def arrive(p):
        main_all(p).wait_recv()
        for s in range(cols):
            at = 8 + half * s
            l32[p + 1, at : at + half] = main[p, s].astype(F32)

    def edge_arrive(dr):
        relay_copy(dr).wait_recv()
        there, q, r = (top, 0, 3) if dr > 0 else (bot, chunks + 1, 0)
        for t in range(4):
            at = 8 + quarter * t
            l32[q, at : at + quarter, r * width : (r + 1) * width] = there[:, t * width : (t + 1) * width].astype(F32)

    between = has_up & has_down
    arrive(1)
    arrive(early)
    pl.when(flip)(lambda: relay(1))
    pl.when(jnp.logical_not(flip) & has_up)(lambda: relay(-1))
    shift(early + 1)
    shift(jnp.where(flip, 0, chunks + 1))
    for p in range(2, chunks - 1):
        arrive(p)
    edge_all().wait_recv()
    for s in range(cols):
        for p in range(1, chunks - 1):
            for k, j in enumerate((0, half - 1)):
                at = 8 + half * s + j
                l32[p + 1, at : at + 1] = main_e[s, 2 * (p - 1) + k : 2 * (p - 1) + k + 1].astype(F32)
    for p in range(1, chunks - 1):
        shift(p + 1)
    pl.when(has_up & jnp.logical_not(between))(lambda: edge_arrive(1))
    pl.when(has_down & jnp.logical_not(between))(lambda: edge_arrive(-1))
    shift(jnp.where(flip, chunks + 1, 0))
    arrive(late)
    shift(late + 1)

    @pl.when(between)
    def _():
        relay(1)
        edge_arrive(1)
        edge_arrive(-1)
        shift(0)
        shift(chunks + 1)

    for copy, item in zip(copies, plan):
        pl.when(item[4])(copy.wait_send)
    for p in range(chunks):
        main_all(p).wait_send()
    edge_all().wait_send()
    pl.when(has_down)(lambda: relay_copy(1).wait_send())
    pl.when(has_up)(lambda: relay_copy(-1).wait_send())


def finish(shifted, band, b3, out):
    chunks, full, quad = shifted.shape[1] - 2, shifted.shape[2], shifted.shape[3]
    bias3 = jnp.concatenate([b3[...]] * 8, axis=1)
    for q in range(chunks // 2):
        acc = None
        for b in range(3):
            lhs = jnp.concatenate([shifted[b, 2 * q + t] for t in range(4)], axis=1)
            part = dot(lhs, band[b])
            acc = part if acc is None else acc + part
        out[8 * q : 8 * q + 8] = (acc + bias3).astype(BF16).T.reshape(8, quad // 4, full)


def on_device(rows, cols, features, conv_one, bias_one, conv_two, bias_two, conv_three, bias_three):
    tr, tc, ch = features.shape
    c2 = conv_two.shape[3]
    width = conv_three.shape[3]
    half, orow = tc // 2, tr // 2
    full, quad = cols * half, 4 * width
    vmem = pl.BlockSpec(memory_space=pltpu.VMEM)
    hbm = pl.BlockSpec(memory_space=pltpu.HBM)
    dma = pltpu.SemaphoreType.DMA
    shifted, band = pl.pallas_call(
        functools.partial(kernel, rows, cols),
        out_shape=[
            pltpu.VMEM((3, orow // 4 + 2, full, quad), BF16),
            pltpu.VMEM((3, 4 * quad, 2 * quad), BF16),
        ],
        in_specs=[hbm] * 6,
        out_specs=[vmem, vmem],
        scratch_shapes=[
            pltpu.VMEM(features.shape, BF16),
            pltpu.VMEM(conv_one.shape, BF16),
            pltpu.VMEM((1, ch), F32),
            pltpu.VMEM(conv_two.shape, BF16),
            pltpu.VMEM((1, c2), F32),
            pltpu.VMEM(conv_three.shape, BF16),
            pltpu.VMEM((ch // 128, tr + 4, tc + 24, 128), F32),
            pltpu.VMEM((tr, 2, ch), BF16),
            pltpu.VMEM((tr, 2, ch), BF16),
            pltpu.VMEM((tr + 3, 2, ch), BF16),
            pltpu.VMEM((tr + 3, 2, ch), BF16),
            pltpu.VMEM((2, tc, ch), BF16),
            pltpu.VMEM((1, tc, ch), BF16),
            pltpu.VMEM((tr + 4, 32, 4 * ch), BF16),
            pltpu.VMEM((tr + 1, 32, 3 * ch), BF16),
            pltpu.VMEM((orow, 32, c2), F32),
            pltpu.VMEM((orow // 4, cols, half, quad), BF16),
            pltpu.VMEM((orow // 4, cols, half, quad), BF16),
            pltpu.VMEM((full // 4, quad), BF16),
            pltpu.VMEM((full // 4, quad), BF16),
            pltpu.VMEM((full // 4, quad), BF16),
            pltpu.VMEM((full // 4, quad), BF16),
            pltpu.VMEM((orow // 4 + 2, full + 16, quad), F32),
            pltpu.VMEM((tr - 12, 8, 4 * ch), F32),
            pltpu.VMEM((orow // 2 + 1, 2, 8, 3 * ch), F32),
            pltpu.VMEM((orow // 2, 8, c2), F32),
            pltpu.VMEM((cols, orow // 2 - 4, quad), BF16),
            pltpu.VMEM((cols, orow // 2 - 4, quad), BF16),
            dma((8,)), dma((8,)), dma((8,)), dma((orow // 4,)), dma((orow // 4,)), dma((2,)), dma((2,)), dma, dma,
        ],
        compiler_params=pltpu.CompilerParams(
            collective_id=0, has_side_effects=True, vmem_limit_bytes=58 * 1024 * 1024
        ),
    )(
        features, conv_one, bias_one.reshape(1, -1), conv_two, bias_two.reshape(1, -1), conv_three,
    )
    return pl.pallas_call(
        finish,
        out_shape=jax.ShapeDtypeStruct((orow, width, full), BF16),
        in_specs=[vmem] * 3,
        out_specs=vmem,
        compiler_params=pltpu.CompilerParams(vmem_limit_bytes=24 * 1024 * 1024),
    )(shifted, band, bias_three.reshape(1, -1))


def solution(mesh):
    in_specs = (
        P("row", "col", None),
        P(),
        P(),
        P(),
        P(),
        P("col", None, None, None, None),
        P("col"),
    )
    return jax.shard_map(
        functools.partial(on_device, mesh.shape["row"], mesh.shape["col"]),
        mesh=mesh, in_specs=in_specs, out_specs=P("row", "col", None), check_vma=False,
    )
```

```python
import functools

import jax
import jax.numpy as jnp
from jax import lax
from jax.experimental import pallas as pl
from jax.experimental.pallas import tpu as pltpu
from jax.sharding import PartitionSpec as P

MESH = pl.DeviceIdType.MESH
F32 = jnp.float32
BF16 = jnp.bfloat16


def dot(a, b):
    return jnp.dot(a, b, preferred_element_type=F32)


def kernel(
    rows, cols,
    feat_hbm, w1_hbm, b1_hbm, w2_hbm, b2_hbm, w3_hbm, b3_hbm, shifted, band, value,
    feat, w1, b1, w2, b2, w3, b3, x32, st_l, st_r, rc_l, rc_r, rc_u, rc_d, taps, a2, l2, send, main,
    high, low, top, bot, l32,
    e32, a2e, l2e, send_e, main_e, total,
    w_sem, h_send, h_recv, m_send, m_recv, r_send, r_recv, e_send, e_recv,
):
    row = lax.axis_index("row")
    col = lax.axis_index("col")
    tr, tc, ch = feat.shape
    half = tc // 2
    has_up, has_down = row > 0, row < rows - 1
    has_left, has_right = col > 0, col < cols - 1

    lo, hi = 6, 18
    load_mid, load_w3, load_b1, load_one, load_b2, load_two, load_low, load_high, load_b3 = [
        pltpu.make_async_copy(src, dst, w_sem.at[index])
        for index, (src, dst) in enumerate(
            (
                (feat_hbm.at[lo:hi], feat.at[lo:hi]), (w3_hbm, w3), (b1_hbm, b1),
                (w1_hbm, w1), (b2_hbm, b2), (w2_hbm, w2),
                (feat_hbm.at[0:lo], feat.at[0:lo]), (feat_hbm.at[hi:tr], feat.at[hi:tr]), (b3_hbm, b3),
            )
        )
    ]
    barrier = pltpu.get_barrier_semaphore()

    def greet(device_row, device_col):
        pl.semaphore_signal(barrier, inc=1, device_id=(device_row, device_col), device_id_type=MESH)

    part = cols // 2
    own = col // part

    zone = cols // 4
    mine = col // zone
    span = [[t * zone + lax.rem(col + k, 2) + 2 * (k // 2) for k in range(zone)] for t in (2 - 2 * own, 3 - 2 * own)]
    span.append([(2 * own + 1 - lax.rem(mine, 2)) * zone + lax.rem(col + k, 2) + 2 * (k // 2) for k in range(zone)])
    span.append([mine * zone + lax.rem(col + k, zone) for k in range(1, zone)])
    first_part, rest = span[0][:2] + span[2][:2] + span[3], span[0][2:] + span[2][2:] + span[1]

    reach = cols - 1
    for d in span[0]:
        greet(row, d)
    load_mid.start()
    for d in span[1]:
        greet(row, d)
    for there, dr in ((has_up, -1), (has_down, 1)):
        for beside, dc in ((True, 0), (has_left, -1), (has_right, 1)):
            pl.when(there & beside)(functools.partial(greet, row + dr, col + dc))
            reach = reach + (there & beside).astype(jnp.int32)
    for d in span[2] + span[3]:
        greet(row, d)
    for load in (load_one, load_b1, load_low, load_high):
        load.start()
    lanes_of = [slice(128 * h, 128 * h + 128) for h in range(ch // 128)]

    def widen(first, last):
        for h, part in enumerate(lanes_of):
            x32[h, first + 2 : last + 2, 8 : tc + 8, :] = feat[first:last, :, part].astype(F32)

    def make_taps(first, count):
        for j in range(4):
            for h in range(ch // 128):
                taps[pl.ds(first, count), :, j * ch + 128 * h : j * ch + 128 * h + 128] = x32[
                    h, pl.ds(first, count), pl.ds(j + 6, 32, stride=2), :
                ].astype(BF16)

    load_mid.wait()
    for load in (load_b2, load_two, load_w3, load_b3):
        load.start()
    widen(lo, hi)
    make_taps(lo + 2, hi - lo)

    zero = lambda ref, lo, hi: ref.__setitem__(
        slice(lo, hi), jnp.zeros((hi - lo,) + ref.shape[1:], ref.dtype)
    )
    copies = []
    plan = (
        (feat.at[tr - 2 : tr], rc_u, 1, 0, has_down, has_up, (rc_u, 0, 2)),
        (feat.at[0:1], rc_d, -1, 0, has_up, has_down, (rc_d, 0, 1)),
        (st_r, rc_l.at[2 : tr + 2], 0, 1, has_right, has_left, (rc_l, 2, tr + 2)),
        (st_l, rc_r.at[2 : tr + 2], 0, -1, has_left, has_right, (rc_r, 2, tr + 2)),
        (st_r.at[tr - 2 : tr], rc_l.at[0:2], 1, 1, has_down & has_right, has_up & has_left, (rc_l, 0, 2)),
        (st_r.at[0:1], rc_l.at[tr + 2 : tr + 3], -1, 1, has_up & has_right, has_down & has_left, (rc_l, tr + 2, tr + 3)),
        (st_l.at[tr - 2 : tr], rc_r.at[0:2], 1, -1, has_down & has_left, has_up & has_right, (rc_r, 0, 2)),
        (st_l.at[0:1], rc_r.at[tr + 2 : tr + 3], -1, -1, has_up & has_left, has_down & has_right, (rc_r, tr + 2, tr + 3)),
    )
    for index, (src, dst, dr, dc, sends, gets, hole) in enumerate(plan):
        copy = pltpu.make_async_remote_copy(
            src_ref=src, dst_ref=dst, send_sem=h_send.at[index], recv_sem=h_recv.at[index],
            device_id=(row + dr, col + dc), device_id_type=MESH,
        )
        copies.append(copy)
        pl.when(jnp.logical_not(gets))(functools.partial(zero, *hole))

    width = w3.shape[3]
    quad = 4 * width
    full = cols * half
    quarter = full // 4
    chunks = main.shape[0]

    inner = 8 * (chunks - 2)
    load_b1.wait()
    load_one.wait()
    bias1 = b1[...]
    left_edge = jnp.logical_not(has_left)
    out_ch = w2.shape[3]

    def first_layer(first, lines):
        m = lines * 32
        for parity in range(2):
            acc = None
            for a in range(3):
                lhs = taps[pl.ds(first + a, lines), :, parity * ch : (parity + 3) * ch]
                part = dot(lhs.reshape(m, 3 * ch), w1[a].reshape(3 * ch, ch))
                acc = part if acc is None else acc + part
            acc = jnp.maximum(acc + bias1, 0.0)
            if parity == 0:
                spot = lax.broadcasted_iota(jnp.int32, acc.shape, 0)
                acc = jnp.where((lax.rem(spot, 32) == 0) & left_edge, 0.0, acc)
                moved = pltpu.roll(acc, m - 1, 0)
                a2[pl.ds(first, lines), :, 2 * ch : 3 * ch] = moved.astype(BF16).reshape(lines, 32, ch)
            a2[pl.ds(first, lines), :, parity * ch : (parity + 1) * ch] = acc.astype(BF16).reshape(lines, 32, ch)

    def second_layer(first, count):
        acc = None
        for a in range(3):
            lhs = jnp.concatenate([a2[2 * (first + i) + a] for i in range(count)], axis=0)
            part = dot(lhs, w2[a].reshape(3 * ch, out_ch))
            acc = part if acc is None else acc + part
        l2[pl.ds(first, count)] = jnp.maximum(acc + b2[...], 0.0).reshape(count, 32, out_ch)

    def pack(p):
        for g in range(cols):
            piece = jnp.concatenate(
                [l2[4 * p + r, 0:half, g * width : (g + 1) * width] for r in range(4)], axis=1
            )
            send[p, g] = piece.astype(BF16)

    def main_copy(p, d):
        return pltpu.make_async_remote_copy(
            src_ref=send.at[p, d], dst_ref=main.at[p, col], send_sem=m_send.at[p],
            recv_sem=m_recv.at[p], device_id=(row, d), device_id_type=MESH,
        )

    def main_all(p):
        others = pl.ds(0, cols - 1)
        return pltpu.make_async_remote_copy(
            src_ref=send.at[p, others], dst_ref=main.at[p, others], send_sem=m_send.at[p],
            recv_sem=m_recv.at[p], device_id=(row, lax.rem(col + 1, cols)), device_id_type=MESH,
        )

    def send_out(p, devices):
        for d in devices:
            main_copy(p, d).start()

    flip = has_down & jnp.logical_not(has_up)
    early = jnp.where(flip, chunks - 1, 0)
    late = chunks - 1 - early

    def clear_top():
        a2[0] = jnp.zeros(a2.shape[1:], BF16)

    def emit(p):
        second_layer(4 * p, 4)
        pack(p)

    def edge_layers():
        base, picks = 8, 4
        far_j = 6 + 2 * (half + 1 - picks)
        for j in range(4):
            for h in range(ch // 128):
                lanes = slice(j * ch + 128 * h, j * ch + 128 * h + 128)
                for at, there in ((6, 0), (far_j, picks)):
                    e32[:, there : there + picks, lanes] = x32[
                        h, base : base + inner + 4, pl.ds(j + at, picks, stride=2), :
                    ]
        n = inner + 2
        m = n * 8
        for parity in range(2):
            acc = None
            for a in range(3):
                lhs = e32[a : a + n, :, parity * ch : (parity + 3) * ch].reshape(m, 3 * ch).astype(BF16)
                part = dot(lhs, w1[a].reshape(3 * ch, ch))
                acc = part if acc is None else acc + part
            acc = jnp.maximum(acc + bias1, 0.0)
            if parity == 0:
                spot = lax.broadcasted_iota(jnp.int32, acc.shape, 0)
                acc = jnp.where((lax.rem(spot, 8) == 0) & left_edge, 0.0, acc)
                a2e[:, :, :, 2 * ch : 3 * ch] = pltpu.roll(acc, m - 1, 0).reshape(n // 2, 2, 8, ch)
            a2e[:, :, :, parity * ch : (parity + 1) * ch] = acc.reshape(n // 2, 2, 8, ch)
        count = inner // 2
        acc = None
        for a in range(3):
            lhs = a2e[a // 2 : a // 2 + count, a % 2].reshape(count * 8, 3 * ch).astype(BF16)
            part = dot(lhs, w2[a].reshape(3 * ch, out_ch))
            acc = part if acc is None else acc + part
        l2e[...] = jnp.maximum(acc + b2[...], 0.0).reshape(count, 8, out_ch)
        for g in range(cols):
            lanes = slice(g * width, (g + 1) * width)
            lines = [
                jnp.concatenate([l2e[4 * p + r, j : j + 1, lanes] for r in range(4)], axis=1)
                for p in range(chunks - 2) for j in (0, 6)
            ]
            send_e[g] = jnp.concatenate(lines, axis=0).astype(BF16)

    def edge_copy(d):
        return pltpu.make_async_remote_copy(
            src_ref=send_e.at[d], dst_ref=main_e.at[col], send_sem=e_send, recv_sem=e_recv,
            device_id=(row, d), device_id_type=MESH,
        )

    def edge_all():
        others = pl.ds(0, cols - 1)
        return pltpu.make_async_remote_copy(
            src_ref=send_e.at[others], dst_ref=main_e.at[others], send_sem=e_send, recv_sem=e_recv,
            device_id=(row, lax.rem(col + 1, cols)), device_id_type=MESH,
        )

    def send_edges(devices):
        for d in devices:
            edge_copy(d).start()

    for p in range(1, chunks - 1):
        if p > 1:
            make_taps(hi + 2 + 8 * (p - 2), 8)
        first_layer(8 * p + (p > 1), 8 + (p == 1))
        if p == 1:
            load_low.wait()
            load_high.wait()
            widen(0, lo)
            widen(hi, tr)
            for h, part in enumerate(lanes_of):
                st_r[:, :, part] = x32[h, 2 : tr + 2, tc + 6 : tc + 8, :].astype(BF16)
                st_l[:, :, part] = x32[h, 2 : tr + 2, 8:10, :].astype(BF16)
            pl.semaphore_wait(barrier, reach)
            for copy, item in zip(copies, plan):
                pl.when(item[4])(copy.start)
            load_b2.wait()
            load_two.wait()
        emit(p)
        send_out(p, first_part + rest)
        main[p, col] = send[p, col]

    for copy, item in zip(copies, plan):
        pl.when(item[5])(copy.wait_recv)
    for h, part in enumerate(lanes_of):
        x32[h, 0:2, 8 : tc + 8, :] = rc_u[:, :, part].astype(F32)
        x32[h, tr + 2 : tr + 3, 8 : tc + 8, :] = rc_d[:, :, part].astype(F32)
        x32[h, 0 : tr + 3, 6:8, :] = rc_l[:, :, part].astype(F32)
        x32[h, 0 : tr + 3, tc + 8 : tc + 10, :] = rc_r[:, :, part].astype(F32)

    for p in (early, late):
        make_taps(8 * p, 12)
        first_layer(8 * p, 9)
        pl.when(jnp.logical_not(has_up))(clear_top)
        emit(p)
        send_out(p, first_part + rest)
        main[p, col] = send[p, col]
        if p is early:
            edge_layers()
            send_edges(first_part + rest)
            main_e[col] = send_e[col]

    load_w3.wait()
    load_b3.wait()
    band[...] = jnp.zeros_like(band)
    for b in range(3):
        for a in range(3):
            block = w3[0, a, b]
            for i in range(8):
                at = (i + 3 + a) * width
                band[b, at : at + width, i * width : (i + 1) * width] = block
    for q in range(chunks + 2):
        l32[q, 0:8] = jnp.zeros((8, quad), F32)
        l32[q, full + 8 : full + 16] = jnp.zeros((8, quad), F32)
    for q in (0, chunks + 1):
        l32[q, 8 : full + 8] = jnp.zeros((full, quad), F32)


    def relay_copy(dr):
        src, there, index = (high, top, 0) if dr > 0 else (low, bot, 1)
        return pltpu.make_async_remote_copy(
            src_ref=src, dst_ref=there, send_sem=r_send.at[index], recv_sem=r_recv.at[index],
            device_id=(row + dr, col), device_id_type=MESH,
        )

    def relay(dr):
        there, q, r = (high, chunks, 3) if dr > 0 else (low, 1, 0)
        pieces = [l32[q, 8 + quarter * t : 8 + quarter * (t + 1), r * width : (r + 1) * width] for t in range(4)]
        there[...] = jnp.concatenate(pieces, axis=1).astype(BF16)
        relay_copy(dr).start()

    def shift(q):
        for b in range(3):
            shifted[b, q] = l32[q, 7 + b : 7 + b + full].astype(BF16)

    def arrive(p):
        main_all(p).wait_recv()
        for s in range(cols):
            at = 8 + half * s
            l32[p + 1, at : at + half] = main[p, s].astype(F32)

    def edge_arrive(dr):
        relay_copy(dr).wait_recv()
        there, q, r = (top, 0, 3) if dr > 0 else (bot, chunks + 1, 0)
        for t in range(4):
            at = 8 + quarter * t
            l32[q, at : at + quarter, r * width : (r + 1) * width] = there[:, t * width : (t + 1) * width].astype(F32)

    begin = jnp.where(flip, chunks - 2, 0)

    def third_dots(tile, count):
        rows_of = pl.ds(pl.multiple_of(tile * quad, quad), count * quad)
        acc = None
        for b in range(3):
            lhs = jnp.concatenate([shifted[b, begin + tile + t] for t in range(count)], axis=1)
            part = dot(lhs, band[b, rows_of])
            acc = part if acc is None else acc + part
        return acc

    def third_start():
        total[...] = third_dots(jnp.where(flip, 0, 1), 3) + jnp.concatenate([b3[...]] * 8, axis=1)

    def third_end():
        acc = total[...] + third_dots(jnp.where(flip, 3, 0), 1)
        value[...] = acc.astype(BF16).T.reshape(8, width, full)

    between = has_up & has_down
    arrive(1)
    arrive(early)
    pl.when(flip)(lambda: relay(1))
    pl.when(jnp.logical_not(flip) & has_up)(lambda: relay(-1))
    shift(early + 1)
    shift(jnp.where(flip, 0, chunks + 1))
    for p in range(2, chunks - 1):
        arrive(p)
    edge_all().wait_recv()
    for s in range(cols):
        for p in range(1, chunks - 1):
            for k, j in enumerate((0, half - 1)):
                at = 8 + half * s + j
                l32[p + 1, at : at + 1] = main_e[s, 2 * (p - 1) + k : 2 * (p - 1) + k + 1].astype(F32)
    for p in range(1, chunks - 1):
        shift(p + 1)
    third_start()
    pl.when(has_up & jnp.logical_not(between))(lambda: edge_arrive(1))
    pl.when(has_down & jnp.logical_not(between))(lambda: edge_arrive(-1))
    shift(jnp.where(flip, chunks + 1, 0))
    pl.when(jnp.logical_not(between))(third_end)
    arrive(late)
    shift(late + 1)

    @pl.when(between)
    def _():
        relay(1)
        edge_arrive(1)
        edge_arrive(-1)
        shift(0)
        shift(chunks + 1)
        third_end()

    for copy, item in zip(copies, plan):
        pl.when(item[4])(copy.wait_send)
    for p in range(chunks):
        main_all(p).wait_send()
    edge_all().wait_send()
    pl.when(has_down)(lambda: relay_copy(1).wait_send())
    pl.when(has_up)(lambda: relay_copy(-1).wait_send())


def finish(rows, shifted, band, b3, value, out, half, sems):
    chunks, full, quad = shifted.shape[1] - 2, shifted.shape[2], shifted.shape[3]
    flip = (lax.axis_index("row") == 0) & (rows > 1)
    early = pl.ds(8 * jnp.where(flip, 1, 0), 8)
    late = pl.ds(8 * jnp.where(flip, 0, 1), 8)
    q = jnp.where(flip, 0, chunks - 2)
    first = pltpu.make_async_copy(value, out.at[early], sems.at[0])
    first.start()
    bias3 = jnp.concatenate([b3[...]] * 8, axis=1)
    acc = None
    for b in range(3):
        lhs = jnp.concatenate([shifted[b, q + t] for t in range(4)], axis=1)
        part = dot(lhs, band[b])
        acc = part if acc is None else acc + part
    half[...] = (acc + bias3).astype(BF16).T.reshape(8, quad // 4, full)
    second = pltpu.make_async_copy(half, out.at[late], sems.at[1])
    second.start()
    first.wait()
    second.wait()


def on_device(rows, cols, features, conv_one, bias_one, conv_two, bias_two, conv_three, bias_three):
    tr, tc, ch = features.shape
    c2 = conv_two.shape[3]
    width = conv_three.shape[3]
    half, orow = tc // 2, tr // 2
    full, quad = cols * half, 4 * width
    vmem = pl.BlockSpec(memory_space=pltpu.VMEM)
    hbm = pl.BlockSpec(memory_space=pltpu.HBM)
    dma = pltpu.SemaphoreType.DMA
    shifted, band, value = pl.pallas_call(
        functools.partial(kernel, rows, cols),
        out_shape=[
            pltpu.VMEM((3, orow // 4 + 2, full, quad), BF16),
            pltpu.VMEM((3, 4 * quad, 2 * quad), BF16),
            pltpu.VMEM((8, width, full), BF16),
        ],
        in_specs=[hbm] * 7,
        out_specs=[vmem] * 3,
        scratch_shapes=[
            pltpu.VMEM(features.shape, BF16),
            pltpu.VMEM(conv_one.shape, BF16),
            pltpu.VMEM((1, ch), F32),
            pltpu.VMEM(conv_two.shape, BF16),
            pltpu.VMEM((1, c2), F32),
            pltpu.VMEM(conv_three.shape, BF16),
            pltpu.VMEM((1, width), F32),
            pltpu.VMEM((ch // 128, tr + 4, tc + 24, 128), F32),
            pltpu.VMEM((tr, 2, ch), BF16),
            pltpu.VMEM((tr, 2, ch), BF16),
            pltpu.VMEM((tr + 3, 2, ch), BF16),
            pltpu.VMEM((tr + 3, 2, ch), BF16),
            pltpu.VMEM((2, tc, ch), BF16),
            pltpu.VMEM((1, tc, ch), BF16),
            pltpu.VMEM((tr + 4, 32, 4 * ch), BF16),
            pltpu.VMEM((tr + 1, 32, 3 * ch), BF16),
            pltpu.VMEM((orow, 32, c2), F32),
            pltpu.VMEM((orow // 4, cols, half, quad), BF16),
            pltpu.VMEM((orow // 4, cols, half, quad), BF16),
            pltpu.VMEM((full // 4, quad), BF16),
            pltpu.VMEM((full // 4, quad), BF16),
            pltpu.VMEM((full // 4, quad), BF16),
            pltpu.VMEM((full // 4, quad), BF16),
            pltpu.VMEM((orow // 4 + 2, full + 16, quad), F32),
            pltpu.VMEM((tr - 12, 8, 4 * ch), F32),
            pltpu.VMEM((orow // 2 + 1, 2, 8, 3 * ch), F32),
            pltpu.VMEM((orow // 2, 8, c2), F32),
            pltpu.VMEM((cols, orow // 2 - 4, quad), BF16),
            pltpu.VMEM((cols, orow // 2 - 4, quad), BF16),
            pltpu.VMEM((full, 2 * quad), F32),
            dma((9,)), dma((8,)), dma((8,)), dma((orow // 4,)), dma((orow // 4,)), dma((2,)), dma((2,)), dma, dma,
        ],
        compiler_params=pltpu.CompilerParams(
            collective_id=0, has_side_effects=True, vmem_limit_bytes=58 * 1024 * 1024
        ),
    )(
        features, conv_one, bias_one.reshape(1, -1), conv_two, bias_two.reshape(1, -1),
        conv_three, bias_three.reshape(1, -1),
    )
    return pl.pallas_call(
        functools.partial(finish, rows),
        out_shape=jax.ShapeDtypeStruct((orow, width, full), BF16),
        in_specs=[vmem] * 4,
        out_specs=hbm,
        scratch_shapes=[pltpu.VMEM((8, width, full), BF16), dma((2,))],
        compiler_params=pltpu.CompilerParams(vmem_limit_bytes=24 * 1024 * 1024),
    )(shifted, band, bias_three.reshape(1, -1), value)


def solution(mesh):
    in_specs = (
        P("row", "col", None),
        P(),
        P(),
        P(),
        P(),
        P("col", None, None, None, None),
        P("col"),
    )
    return jax.shard_map(
        functools.partial(on_device, mesh.shape["row"], mesh.shape["col"]),
        mesh=mesh, in_specs=in_specs, out_specs=P("row", "col", None), check_vma=False,
    )
```

```python
import functools

import jax
import jax.numpy as jnp
from jax import lax
from jax.experimental import pallas as pl
from jax.experimental.pallas import tpu as pltpu
from jax.sharding import PartitionSpec as P

MESH = pl.DeviceIdType.MESH
F32 = jnp.float32
BF16 = jnp.bfloat16


def dot(a, b):
    return jnp.dot(a, b, preferred_element_type=F32)


def kernel(
    rows, cols,
    feat_hbm, w1_hbm, b1_hbm, w2_hbm, b2_hbm, w3_hbm, b3_hbm, shifted, band, value, partial,
    feat, w1, b1, w2, b2, w3, b3, x32, st_l, st_r, rc_l, rc_r, rc_u, rc_d, taps, a2, l2, send, main,
    high, low, top, bot, l32,
    e32, a2e, l2e, send_e, main_e, total,
    w_sem, h_send, h_recv, m_send, m_recv, r_send, r_recv, e_send, e_recv,
):
    row = lax.axis_index("row")
    col = lax.axis_index("col")
    tr, tc, ch = feat.shape
    half = tc // 2
    has_up, has_down = row > 0, row < rows - 1
    has_left, has_right = col > 0, col < cols - 1

    lo, hi = 6, 18
    load_mid, load_w3, load_b1, load_one, load_b2, load_two, load_low, load_high, load_b3 = [
        pltpu.make_async_copy(src, dst, w_sem.at[index])
        for index, (src, dst) in enumerate(
            (
                (feat_hbm.at[lo:hi], feat.at[lo:hi]), (w3_hbm, w3), (b1_hbm, b1),
                (w1_hbm, w1), (b2_hbm, b2), (w2_hbm, w2),
                (feat_hbm.at[0:lo], feat.at[0:lo]), (feat_hbm.at[hi:tr], feat.at[hi:tr]), (b3_hbm, b3),
            )
        )
    ]
    barrier = pltpu.get_barrier_semaphore()

    def greet(device_row, device_col):
        pl.semaphore_signal(barrier, inc=1, device_id=(device_row, device_col), device_id_type=MESH)

    part = cols // 2
    own = col // part

    zone = cols // 4
    mine = col // zone
    span = [[t * zone + lax.rem(col + k, 2) + 2 * (k // 2) for k in range(zone)] for t in (2 - 2 * own, 3 - 2 * own)]
    span.append([(2 * own + 1 - lax.rem(mine, 2)) * zone + lax.rem(col + k, 2) + 2 * (k // 2) for k in range(zone)])
    span.append([mine * zone + lax.rem(col + k, zone) for k in range(1, zone)])
    first_part, rest = span[0][:2] + span[2][:2] + span[3], span[0][2:] + span[2][2:] + span[1]

    reach = cols - 1
    for d in span[0]:
        greet(row, d)
    load_mid.start()
    load_one.start()
    for d in span[1]:
        greet(row, d)
    for there, dr in ((has_up, -1), (has_down, 1)):
        for beside, dc in ((True, 0), (has_left, -1), (has_right, 1)):
            pl.when(there & beside)(functools.partial(greet, row + dr, col + dc))
            reach = reach + (there & beside).astype(jnp.int32)
    for d in span[2] + span[3]:
        greet(row, d)
    for load in (load_b1, load_low, load_high):
        load.start()
    lanes_of = [slice(128 * h, 128 * h + 128) for h in range(ch // 128)]

    def widen(first, last):
        for h, part in enumerate(lanes_of):
            x32[h, first + 2 : last + 2, 8 : tc + 8, :] = feat[first:last, :, part].astype(F32)

    def make_taps(first, count):
        for j in range(4):
            for h in range(ch // 128):
                taps[pl.ds(first, count), :, j * ch + 128 * h : j * ch + 128 * h + 128] = x32[
                    h, pl.ds(first, count), pl.ds(j + 6, 32, stride=2), :
                ].astype(BF16)

    load_mid.wait()
    for load in (load_b2, load_two, load_w3, load_b3):
        load.start()
    widen(lo, hi)
    make_taps(lo + 2, hi - lo)

    zero = lambda ref, lo, hi: ref.__setitem__(
        slice(lo, hi), jnp.zeros((hi - lo,) + ref.shape[1:], ref.dtype)
    )
    copies = []
    plan = (
        (feat.at[tr - 2 : tr], rc_u, 1, 0, has_down, has_up, (rc_u, 0, 2)),
        (feat.at[0:1], rc_d, -1, 0, has_up, has_down, (rc_d, 0, 1)),
        (st_r, rc_l.at[2 : tr + 2], 0, 1, has_right, has_left, (rc_l, 2, tr + 2)),
        (st_l, rc_r.at[2 : tr + 2], 0, -1, has_left, has_right, (rc_r, 2, tr + 2)),
        (st_r.at[tr - 2 : tr], rc_l.at[0:2], 1, 1, has_down & has_right, has_up & has_left, (rc_l, 0, 2)),
        (st_r.at[0:1], rc_l.at[tr + 2 : tr + 3], -1, 1, has_up & has_right, has_down & has_left, (rc_l, tr + 2, tr + 3)),
        (st_l.at[tr - 2 : tr], rc_r.at[0:2], 1, -1, has_down & has_left, has_up & has_right, (rc_r, 0, 2)),
        (st_l.at[0:1], rc_r.at[tr + 2 : tr + 3], -1, -1, has_up & has_left, has_down & has_right, (rc_r, tr + 2, tr + 3)),
    )
    for index, (src, dst, dr, dc, sends, gets, hole) in enumerate(plan):
        copy = pltpu.make_async_remote_copy(
            src_ref=src, dst_ref=dst, send_sem=h_send.at[index], recv_sem=h_recv.at[index],
            device_id=(row + dr, col + dc), device_id_type=MESH,
        )
        copies.append(copy)
        pl.when(jnp.logical_not(gets))(functools.partial(zero, *hole))

    width = w3.shape[3]
    quad = 4 * width
    full = cols * half
    quarter = full // 4
    chunks = main.shape[0]

    inner = 8 * (chunks - 2)
    load_b1.wait()
    load_one.wait()
    bias1 = b1[...]
    left_edge = jnp.logical_not(has_left)
    out_ch = w2.shape[3]

    def first_layer(first, lines):
        m = lines * 32
        for parity in range(2):
            acc = None
            for a in range(3):
                lhs = taps[pl.ds(first + a, lines), :, parity * ch : (parity + 3) * ch]
                part = dot(lhs.reshape(m, 3 * ch), w1[a].reshape(3 * ch, ch))
                acc = part if acc is None else acc + part
            acc = jnp.maximum(acc + bias1, 0.0)
            if parity == 0:
                spot = lax.broadcasted_iota(jnp.int32, acc.shape, 0)
                acc = jnp.where((lax.rem(spot, 32) == 0) & left_edge, 0.0, acc)
                moved = pltpu.roll(acc, m - 1, 0)
                a2[pl.ds(first, lines), :, 2 * ch : 3 * ch] = moved.astype(BF16).reshape(lines, 32, ch)
            a2[pl.ds(first, lines), :, parity * ch : (parity + 1) * ch] = acc.astype(BF16).reshape(lines, 32, ch)

    def second_layer(first, count):
        acc = None
        for a in range(3):
            lhs = jnp.concatenate([a2[2 * (first + i) + a] for i in range(count)], axis=0)
            part = dot(lhs, w2[a].reshape(3 * ch, out_ch))
            acc = part if acc is None else acc + part
        l2[pl.ds(first, count)] = jnp.maximum(acc + b2[...], 0.0).reshape(count, 32, out_ch)

    def pack(p):
        for g in range(cols):
            piece = jnp.concatenate(
                [l2[4 * p + r, 0:half, g * width : (g + 1) * width] for r in range(4)], axis=1
            )
            send[p, g] = piece.astype(BF16)

    def main_copy(p, d):
        return pltpu.make_async_remote_copy(
            src_ref=send.at[p, d], dst_ref=main.at[p, col], send_sem=m_send.at[p],
            recv_sem=m_recv.at[p], device_id=(row, d), device_id_type=MESH,
        )

    def main_all(p):
        others = pl.ds(0, cols - 1)
        return pltpu.make_async_remote_copy(
            src_ref=send.at[p, others], dst_ref=main.at[p, others], send_sem=m_send.at[p],
            recv_sem=m_recv.at[p], device_id=(row, lax.rem(col + 1, cols)), device_id_type=MESH,
        )

    def send_out(p, devices):
        for d in devices:
            main_copy(p, d).start()

    flip = has_down & jnp.logical_not(has_up)
    early = jnp.where(flip, chunks - 1, 0)
    late = chunks - 1 - early

    def clear_top():
        a2[0] = jnp.zeros(a2.shape[1:], BF16)

    def emit(p):
        second_layer(4 * p, 4)
        pack(p)

    def edge_layers():
        base, picks = 8, 4
        far_j = 6 + 2 * (half + 1 - picks)
        for j in range(4):
            for h in range(ch // 128):
                lanes = slice(j * ch + 128 * h, j * ch + 128 * h + 128)
                for at, there in ((6, 0), (far_j, picks)):
                    e32[:, there : there + picks, lanes] = x32[
                        h, base : base + inner + 4, pl.ds(j + at, picks, stride=2), :
                    ]
        n = inner + 2
        m = n * 8
        for parity in range(2):
            acc = None
            for a in range(3):
                lhs = e32[a : a + n, :, parity * ch : (parity + 3) * ch].reshape(m, 3 * ch).astype(BF16)
                part = dot(lhs, w1[a].reshape(3 * ch, ch))
                acc = part if acc is None else acc + part
            acc = jnp.maximum(acc + bias1, 0.0)
            if parity == 0:
                spot = lax.broadcasted_iota(jnp.int32, acc.shape, 0)
                acc = jnp.where((lax.rem(spot, 8) == 0) & left_edge, 0.0, acc)
                a2e[:, :, :, 2 * ch : 3 * ch] = pltpu.roll(acc, m - 1, 0).reshape(n // 2, 2, 8, ch)
            a2e[:, :, :, parity * ch : (parity + 1) * ch] = acc.reshape(n // 2, 2, 8, ch)
        count = inner // 2
        acc = None
        for a in range(3):
            lhs = a2e[a // 2 : a // 2 + count, a % 2].reshape(count * 8, 3 * ch).astype(BF16)
            part = dot(lhs, w2[a].reshape(3 * ch, out_ch))
            acc = part if acc is None else acc + part
        l2e[...] = jnp.maximum(acc + b2[...], 0.0).reshape(count, 8, out_ch)
        for g in range(cols):
            lanes = slice(g * width, (g + 1) * width)
            lines = [
                jnp.concatenate([l2e[4 * p + r, j : j + 1, lanes] for r in range(4)], axis=1)
                for p in range(chunks - 2) for j in (0, 6)
            ]
            send_e[g] = jnp.concatenate(lines, axis=0).astype(BF16)

    def edge_copy(d):
        return pltpu.make_async_remote_copy(
            src_ref=send_e.at[d], dst_ref=main_e.at[col], send_sem=e_send, recv_sem=e_recv,
            device_id=(row, d), device_id_type=MESH,
        )

    def edge_all():
        others = pl.ds(0, cols - 1)
        return pltpu.make_async_remote_copy(
            src_ref=send_e.at[others], dst_ref=main_e.at[others], send_sem=e_send, recv_sem=e_recv,
            device_id=(row, lax.rem(col + 1, cols)), device_id_type=MESH,
        )

    def send_edges(devices):
        for d in devices:
            edge_copy(d).start()

    for p in range(1, chunks - 1):
        if p > 1:
            make_taps(hi + 2 + 8 * (p - 2), 8)
        first_layer(8 * p + (p > 1), 8 + (p == 1))
        if p == 1:
            load_low.wait()
            load_high.wait()
            widen(0, lo)
            widen(hi, tr)
            for h, part in enumerate(lanes_of):
                st_r[:, :, part] = x32[h, 2 : tr + 2, tc + 6 : tc + 8, :].astype(BF16)
                st_l[:, :, part] = x32[h, 2 : tr + 2, 8:10, :].astype(BF16)
            pl.semaphore_wait(barrier, reach)
            for copy, item in zip(copies, plan):
                pl.when(item[4])(copy.start)
            load_b2.wait()
            load_two.wait()
        emit(p)
        send_out(p, first_part + rest)
        main[p, col] = send[p, col]

    for copy, item in zip(copies, plan):
        pl.when(item[5])(copy.wait_recv)
    for h, part in enumerate(lanes_of):
        x32[h, 0:2, 8 : tc + 8, :] = rc_u[:, :, part].astype(F32)
        x32[h, tr + 2 : tr + 3, 8 : tc + 8, :] = rc_d[:, :, part].astype(F32)
        x32[h, 0 : tr + 3, 6:8, :] = rc_l[:, :, part].astype(F32)
        x32[h, 0 : tr + 3, tc + 8 : tc + 10, :] = rc_r[:, :, part].astype(F32)

    for p in (early, late):
        make_taps(8 * p, 12)
        first_layer(8 * p, 9)
        pl.when(jnp.logical_not(has_up))(clear_top)
        emit(p)
        send_out(p, first_part + rest)
        main[p, col] = send[p, col]
        if p is early:
            edge_layers()
            send_edges(first_part + rest)
            main_e[col] = send_e[col]

    load_w3.wait()
    load_b3.wait()
    band[...] = jnp.zeros_like(band)
    for b in range(3):
        for a in range(3):
            block = w3[0, a, b]
            for i in range(8):
                at = (i + 3 + a) * width
                band[b, at : at + width, i * width : (i + 1) * width] = block
    for q in range(chunks + 2):
        l32[q, 0:8] = jnp.zeros((8, quad), F32)
        l32[q, full + 8 : full + 16] = jnp.zeros((8, quad), F32)
    for q in (0, chunks + 1):
        l32[q, 8 : full + 8] = jnp.zeros((full, quad), F32)


    def relay_copy(dr):
        src, there, index = (high, top, 0) if dr > 0 else (low, bot, 1)
        return pltpu.make_async_remote_copy(
            src_ref=src, dst_ref=there, send_sem=r_send.at[index], recv_sem=r_recv.at[index],
            device_id=(row + dr, col), device_id_type=MESH,
        )

    def relay(dr):
        there, p, r = (high, chunks - 1, 3) if dr > 0 else (low, 0, 0)
        lanes = slice(r * width, (r + 1) * width)
        for u in range(zone):
            pieces = [main[p, zone * t + u, :, lanes] for t in range(4)]
            there[u] = jnp.concatenate(pieces, axis=1)
        relay_copy(dr).start()

    def shift(q):
        for b in range(3):
            shifted[b, q] = l32[q, 7 + b : 7 + b + full].astype(BF16)

    def arrive(p, waited=False):
        if not waited:
            main_all(p).wait_recv()
        for s in range(cols):
            at = 8 + half * s
            l32[p + 1, at : at + half] = main[p, s].astype(F32)

    def edge_arrive(dr):
        relay_copy(dr).wait_recv()
        there, q, r = (top, 0, 3) if dr > 0 else (bot, chunks + 1, 0)
        for u in range(zone):
            for t in range(4):
                at = 8 + quarter * t + half * u
                l32[q, at : at + half, r * width : (r + 1) * width] = there[
                    u, :, t * width : (t + 1) * width
                ].astype(F32)

    begin = jnp.where(flip, chunks - 2, 0)

    def third_dots(tile, count):
        rows_of = pl.ds(pl.multiple_of(tile * quad, quad), count * quad)
        acc = None
        for b in range(3):
            lhs = jnp.concatenate([shifted[b, begin + tile + t] for t in range(count)], axis=1)
            part = dot(lhs, band[b, rows_of])
            acc = part if acc is None else acc + part
        return acc

    def third_start():
        total[...] = third_dots(jnp.where(flip, 0, 1), 3) + jnp.concatenate([b3[...]] * 8, axis=1)

    def late_start():
        base = chunks - 2 - begin
        tiles = (0, jnp.where(flip, 2, 1), 3)
        acc = jnp.concatenate([b3[...]] * 8, axis=1)
        for b in range(3):
            lhs = jnp.concatenate([shifted[b, base + t] for t in tiles], axis=1)
            rhs = jnp.concatenate([band[b, pl.ds(pl.multiple_of(t * quad, quad), quad)] for t in tiles], axis=0)
            acc = acc + dot(lhs, rhs)
        partial[...] = acc

    def third_end():
        acc = total[...] + third_dots(jnp.where(flip, 3, 0), 1)
        value[...] = acc.astype(BF16).T.reshape(8, width, full)

    between = has_up & has_down
    arrive(1)
    main_all(early).wait_recv()
    pl.when(flip)(lambda: relay(1))
    pl.when(jnp.logical_not(flip) & has_up)(lambda: relay(-1))
    arrive(early, True)
    shift(early + 1)
    shift(jnp.where(flip, 0, chunks + 1))
    for p in range(2, chunks - 1):
        arrive(p)
    edge_all().wait_recv()
    for s in range(cols):
        for p in range(1, chunks - 1):
            for k, j in enumerate((0, half - 1)):
                at = 8 + half * s + j
                l32[p + 1, at : at + 1] = main_e[s, 2 * (p - 1) + k : 2 * (p - 1) + k + 1].astype(F32)
    for p in range(1, chunks - 1):
        shift(p + 1)
    third_start()
    pl.when(jnp.logical_not(between))(late_start)
    pl.when(has_up & jnp.logical_not(between))(lambda: edge_arrive(1))
    pl.when(has_down & jnp.logical_not(between))(lambda: edge_arrive(-1))
    shift(jnp.where(flip, chunks + 1, 0))
    pl.when(jnp.logical_not(between))(third_end)
    arrive(late)
    shift(late + 1)

    @pl.when(between)
    def _():
        relay(1)
        edge_arrive(1)
        edge_arrive(-1)
        shift(0)
        shift(chunks + 1)
        third_end()
        late_start()

    for copy, item in zip(copies, plan):
        pl.when(item[4])(copy.wait_send)
    for p in range(chunks):
        main_all(p).wait_send()
    edge_all().wait_send()
    pl.when(has_down)(lambda: relay_copy(1).wait_send())
    pl.when(has_up)(lambda: relay_copy(-1).wait_send())


def finish(rows, shifted, band, partial, value, out, half, sems):
    chunks, full, quad = shifted.shape[1] - 2, shifted.shape[2], shifted.shape[3]
    flip = (lax.axis_index("row") == 0) & (rows > 1)
    early = pl.ds(8 * jnp.where(flip, 1, 0), 8)
    late = pl.ds(8 * jnp.where(flip, 0, 1), 8)
    tile = jnp.where(flip, 1, 2)
    rows_of = pl.ds(pl.multiple_of(tile * quad, quad), quad)
    first = pltpu.make_async_copy(value, out.at[early], sems.at[0])
    first.start()
    acc = partial[...]
    for b in range(3):
        acc = acc + dot(shifted[b, jnp.where(flip, 1, chunks)], band[b, rows_of])
    half[...] = acc.astype(BF16).T.reshape(8, quad // 4, full)
    second = pltpu.make_async_copy(half, out.at[late], sems.at[1])
    second.start()
    first.wait()
    second.wait()


def on_device(rows, cols, features, conv_one, bias_one, conv_two, bias_two, conv_three, bias_three):
    tr, tc, ch = features.shape
    c2 = conv_two.shape[3]
    width = conv_three.shape[3]
    half, orow = tc // 2, tr // 2
    full, quad = cols * half, 4 * width
    vmem = pl.BlockSpec(memory_space=pltpu.VMEM)
    hbm = pl.BlockSpec(memory_space=pltpu.HBM)
    dma = pltpu.SemaphoreType.DMA
    shifted, band, value, partial = pl.pallas_call(
        functools.partial(kernel, rows, cols),
        out_shape=[
            pltpu.VMEM((3, orow // 4 + 2, full, quad), BF16),
            pltpu.VMEM((3, 4 * quad, 2 * quad), BF16),
            pltpu.VMEM((8, width, full), BF16),
            pltpu.VMEM((full, 2 * quad), F32),
        ],
        in_specs=[hbm] * 7,
        out_specs=[vmem] * 4,
        scratch_shapes=[
            pltpu.VMEM(features.shape, BF16),
            pltpu.VMEM(conv_one.shape, BF16),
            pltpu.VMEM((1, ch), F32),
            pltpu.VMEM(conv_two.shape, BF16),
            pltpu.VMEM((1, c2), F32),
            pltpu.VMEM(conv_three.shape, BF16),
            pltpu.VMEM((1, width), F32),
            pltpu.VMEM((ch // 128, tr + 4, tc + 24, 128), F32),
            pltpu.VMEM((tr, 2, ch), BF16),
            pltpu.VMEM((tr, 2, ch), BF16),
            pltpu.VMEM((tr + 3, 2, ch), BF16),
            pltpu.VMEM((tr + 3, 2, ch), BF16),
            pltpu.VMEM((2, tc, ch), BF16),
            pltpu.VMEM((1, tc, ch), BF16),
            pltpu.VMEM((tr + 4, 32, 4 * ch), BF16),
            pltpu.VMEM((tr + 1, 32, 3 * ch), BF16),
            pltpu.VMEM((orow, 32, c2), F32),
            pltpu.VMEM((orow // 4, cols, half, quad), BF16),
            pltpu.VMEM((orow // 4, cols, half, quad), BF16),
            pltpu.VMEM((cols // 4, half, quad), BF16),
            pltpu.VMEM((cols // 4, half, quad), BF16),
            pltpu.VMEM((cols // 4, half, quad), BF16),
            pltpu.VMEM((cols // 4, half, quad), BF16),
            pltpu.VMEM((orow // 4 + 2, full + 16, quad), F32),
            pltpu.VMEM((tr - 12, 8, 4 * ch), F32),
            pltpu.VMEM((orow // 2 + 1, 2, 8, 3 * ch), F32),
            pltpu.VMEM((orow // 2, 8, c2), F32),
            pltpu.VMEM((cols, orow // 2 - 4, quad), BF16),
            pltpu.VMEM((cols, orow // 2 - 4, quad), BF16),
            pltpu.VMEM((full, 2 * quad), F32),
            dma((9,)), dma((8,)), dma((8,)), dma((orow // 4,)), dma((orow // 4,)), dma((2,)), dma((2,)), dma, dma,
        ],
        compiler_params=pltpu.CompilerParams(
            collective_id=0, has_side_effects=True, vmem_limit_bytes=58 * 1024 * 1024
        ),
    )(
        features, conv_one, bias_one.reshape(1, -1), conv_two, bias_two.reshape(1, -1),
        conv_three, bias_three.reshape(1, -1),
    )
    return pl.pallas_call(
        functools.partial(finish, rows),
        out_shape=jax.ShapeDtypeStruct((orow, width, full), BF16),
        in_specs=[vmem] * 4,
        out_specs=hbm,
        scratch_shapes=[pltpu.VMEM((8, width, full), BF16), dma((2,))],
        compiler_params=pltpu.CompilerParams(vmem_limit_bytes=24 * 1024 * 1024),
    )(shifted, band, partial, value)


def solution(mesh):
    in_specs = (
        P("row", "col", None),
        P(),
        P(),
        P(),
        P(),
        P("col", None, None, None, None),
        P("col"),
    )
    return jax.shard_map(
        functools.partial(on_device, mesh.shape["row"], mesh.shape["col"]),
        mesh=mesh, in_specs=in_specs, out_specs=P("row", "col", None), check_vma=False,
    )
```
